32 devices in a mesh: row: 4 (over y, core), col: 8 (over z, x).
Axes of the slice: x: 2, y: 2, z: 4, core: 2. Of those that a mesh axis runs over, the one named last changes fastest.
Arguments:
- outside: bfloat16 [2048, 4096], P('row', 'col'), may hold values from 0.0099 to 17.5
- inside_head: bfloat16 [2048, 4096], P('row', 'col'), may hold values from 0.0099 to 17.5
- inside_tail: bfloat16 [2048, 4096], P('row', 'col'), may hold values from 0.0099 to 17.5
- inside_pair: float32 [512, 4096], P(None, 'col'), may hold values from 0.4 to 1.6
- seq_head: int32 [1, 4096], P(None, 'col'), may hold values from 0 to 3
- seq_tail: int32 [1, 4096], P(None, 'col'), may hold values from 0 to 3
- pair_mask: int32 [4, 32], P(None, 'col'), may hold values 0 or 1
- split_weight: float32 [4], replicated, may hold values from 0.5 to 2
- pair_weight: float32 [4, 4], replicated, may hold values from 0.5 to 2
- span_blocks: int32 [1], replicated, may hold values from 8 to 63
- partition: float32 [1], replicated, may hold values from 1 to 3
Outputs:
- outside_out: float32 [2048, 4096], P('row', 'col')
- prob_out: float32 [2048, 4096], P('row', 'col')
The draws below stay inside these ranges and needn't reach their ends.
All inputs are finite; a program needn't handle non-finite values. No bound on the sum of `pair_mask` on one device may be relied on, other than what follows from the above.
Results may differ from the reference program's by a relative error of at most 0.0003.
Values may be sent and summed in bfloat16 or wider, within the bound.
No kernel may reach another device: no remote copies, remote signals or barrier semaphores. Data moves between devices by JAX's collectives and lax.ppermute only.
A program may use at most 64 MiB of HBM per device.

```python
import math
import jax
import jax.numpy as jnp
from jax import lax

BLK = 512
CYC = 1
SUB = 4
BAND_ROWS = 2048
END_NT = 4096
N_ROW = 4
N_COL = 8


def spiked_table(key):
    tile_rows = BAND_ROWS // BLK
    tile_cols = END_NT // BLK
    key_back, key_order, key_height = jax.random.split(key, 3)
    background = jnp.exp(jax.random.uniform(key_back, (BAND_ROWS, END_NT), jnp.float32, jnp.log(0.01), jnp.log(0.2)))
    order_keys = jax.random.split(key_order, tile_rows * tile_cols)
    orders = jax.vmap(lambda subkey: jax.random.permutation(subkey, BLK))(order_keys).reshape(tile_rows, tile_cols, BLK)
    spiked = orders[:, :, :, None] == jnp.arange(BLK, dtype=jnp.int32)[None, None, None, :]
    spiked = spiked.transpose(0, 2, 1, 3).reshape(BAND_ROWS, END_NT)
    height = jax.random.uniform(key_height, (BAND_ROWS, END_NT), jnp.float32, 16.5, 17.5)
    return jnp.where(spiked, height, background).astype(jnp.bfloat16)


def draw_outside(key, part):
    return spiked_table(jax.random.fold_in(key, 101))


def draw_inside_head(key, part):
    return spiked_table(jax.random.fold_in(key, 202))


def draw_inside_tail(key, part):
    return spiked_table(jax.random.fold_in(key, 303))


def place_ends(result, stream_key, low, high):
    longest = result.shape.index(max(result.shape))
    spots = []
    for shift in (0, 1):
        where = [jax.random.randint(jax.random.fold_in(stream_key, axis), (), 0, length) for axis, length in enumerate(result.shape)]
        where[longest] = (where[longest] + shift) % result.shape[longest]
        spots.append(tuple(where))
    return result.at[spots[0]].set(low).at[spots[1]].set(high)


def steps_of(key, extent, cuts, least, top_value):
    def one(axis_at, parts):
        draws = jax.random.uniform(jax.random.fold_in(jax.random.fold_in(key, 6), axis_at), (parts,), jnp.float32, least / len(cuts), top_value / len(cuts))
        return jnp.repeat(jnp.exp(draws), extent[axis_at] // parts).reshape((-1,) + (1,) * (len(extent) - axis_at - 1))

    gain = one(*cuts[0])
    for cut in cuts[1:]:
        gain = gain * one(*cut)
    return gain


def setup_inputs(seed: int = 0) -> dict:
    seeds = jax.random.split(jax.random.key(seed), 12)
    return {
        "outside": draw_outside(jax.random.fold_in(seeds[11], 71), 0),
        "inside_head": draw_inside_head(jax.random.fold_in(seeds[11], 71), 0),
        "inside_tail": draw_inside_tail(jax.random.fold_in(seeds[11], 71), 0),
        "inside_pair": jnp.clip(jnp.exp(math.log(1.6) - 1.3862944 * jax.random.uniform(seeds[3], (CYC * BLK, END_NT), jnp.float32) ** steps_of(seeds[3], (CYC * BLK, END_NT), ((1, 8),), -0.2, 0.2)), 0.4, 1.6),
        "seq_head": place_ends(jax.random.randint(seeds[4], (CYC, END_NT), 0, 4), jax.random.fold_in(seeds[4], 1), 0, 3).astype(jnp.int32),
        "seq_tail": place_ends(jax.random.randint(seeds[5], (CYC, END_NT), 0, 4), jax.random.fold_in(seeds[5], 1), 0, 3).astype(jnp.int32),
        "pair_mask": place_ends((jax.random.randint(seeds[6], (CYC * SUB, N_COL * SUB), 0, 4) < 3).astype(jnp.int32), jax.random.fold_in(seeds[6], 1), 0, 1),
        "split_weight": jnp.clip(jnp.exp(jax.random.uniform(seeds[7], (4,), jnp.float32, math.log(0.5), math.log(2.0))), 0.5, 2.0),
        "pair_weight": jnp.clip(jnp.exp(jax.random.uniform(seeds[8], (4, 4), jnp.float32, math.log(0.5), math.log(2.0))), 0.5, 2.0),
        "span_blocks": jax.random.randint(seeds[9], (1,), N_COL, 8 * N_COL).astype(jnp.int32),
        "partition": jnp.clip(jnp.exp(jax.random.uniform(seeds[10], (1,), jnp.float32, math.log(1.0), math.log(3.0))), 1.0, 3.0),
    }


precise = lax.Precision.HIGHEST

def finish(right_sum, left_sum, head_codes, tail_codes, mask_rows, pair_rows, split_weight, pair_weight, span_blocks, partition, owner_factor):
    cycles, tile_size = head_codes.shape
    repeat = tile_size // mask_rows.shape[1]
    allowed = jnp.repeat(jnp.repeat(mask_rows.astype(jnp.float32), repeat, axis=0), repeat, axis=1).reshape(cycles, tile_size, tile_size)
    letters = jnp.arange(4, dtype=jnp.int32)
    head_hot = (head_codes[:, :, None] == letters[None, None, :]).astype(jnp.float32)
    tail_hot = (tail_codes[:, :, None] == letters[None, None, :]).astype(jnp.float32)
    head_weight = jnp.einsum('mak,k->ma', head_hot, split_weight, precision=precise)
    tail_weight = jnp.einsum('mak,k->ma', tail_hot, split_weight, precision=precise)
    outside_diag = owner_factor * allowed * (right_sum * tail_weight[:, None, :] + head_weight[:, :, None] * left_sum) / tile_size
    pair_table = jnp.einsum('mak,kl,mbl->mab', head_hot, pair_weight, tail_hot, precision=precise)
    positions = jnp.arange(tile_size, dtype=jnp.float32)
    span_nt = tile_size * span_blocks[0].astype(jnp.float32) + positions[None, :] - positions[:, None]
    penalty = jnp.sqrt(64.0 * tile_size / span_nt)
    pair_prob = pair_rows.reshape(cycles, tile_size, tile_size) * outside_diag * pair_table * penalty[None, :, :] / partition[0]
    return (outside_diag.reshape(cycles * tile_size, tile_size), pair_prob.reshape(cycles * tile_size, tile_size))

def row_tiles(array, row_index):
    block = array[row_index * CYC * BLK:(row_index + 1) * CYC * BLK]
    return block.reshape(CYC, BLK, N_COL, BLK).transpose(2, 0, 1, 3).astype(jnp.float32)

def reference(outside, inside_head, inside_tail, inside_pair, seq_head, seq_tail, pair_mask, split_weight, pair_weight, span_blocks, partition):
    col_ids = jnp.arange(N_COL, dtype=jnp.int32)
    right_all = jnp.zeros((N_COL, CYC, BLK, BLK), jnp.float32)
    left_all = jnp.zeros((N_COL, CYC, BLK, BLK), jnp.float32)
    for row_index in range(N_ROW):
        out_tiles = row_tiles(outside, row_index)
        head_tiles = row_tiles(inside_head, row_index)
        tail_tiles = row_tiles(inside_tail, row_index)
        right_term = jnp.einsum('jmac,jmbc->jmab', out_tiles, tail_tiles, precision=precise)
        left_term = jnp.einsum('jmca,jmcb->jmab', head_tiles, out_tiles, precision=precise)
        reach = (col_ids - row_index) % N_ROW
        reach = jnp.where(reach == 0, N_ROW, reach)
        earlier = jnp.concatenate([jnp.zeros_like(left_term[:, :1]), left_term[:, :-1]], axis=1)
        left_all = left_all + jnp.where((col_ids < reach)[:, None, None, None], earlier, left_term)
        window = jnp.zeros_like(right_term)
        for distance in range(1, N_ROW + 1):
            window = window + jnp.roll(right_term, -distance, axis=0)
        right_all = jnp.where((col_ids % N_ROW == row_index)[:, None, None, None], window, right_all)
    outside_out = jnp.zeros(outside.shape, jnp.float32)
    prob_out = jnp.zeros(outside.shape, jnp.float32)
    for col_index in range(N_COL):
        owner_row = col_index % N_ROW
        diag_rows, prob_rows = finish(right_all[col_index], left_all[col_index], seq_head[:, col_index * BLK:(col_index + 1) * BLK], seq_tail[:, col_index * BLK:(col_index + 1) * BLK], pair_mask[:, col_index * SUB:(col_index + 1) * SUB], inside_pair[:, col_index * BLK:(col_index + 1) * BLK], split_weight, pair_weight, span_blocks, partition, 1.0)
        outside_out = outside_out.at[owner_row * CYC * BLK:(owner_row + 1) * CYC * BLK, col_index * BLK:(col_index + 1) * BLK].set(diag_rows)
        prob_out = prob_out.at[owner_row * CYC * BLK:(owner_row + 1) * CYC * BLK, col_index * BLK:(col_index + 1) * BLK].set(prob_rows)
    return (outside_out, prob_out)
```

```python
import jax
import jax.numpy as jnp
from jax import lax
from jax.experimental import pallas as pl
from jax.experimental.pallas import tpu as pltpu
from jax.sharding import PartitionSpec as P


precise = lax.Precision.HIGHEST
VMEM = pl.BlockSpec(memory_space=pltpu.VMEM)
SMEM = pl.BlockSpec(memory_space=pltpu.SMEM)
ANY = pl.BlockSpec(memory_space=pl.ANY)
HBM = pl.BlockSpec(memory_space=pltpu.HBM)
CHUNKS = 4
PARAMS = pltpu.CompilerParams(vmem_limit_bytes=16 << 20)


def encode(x):
    y = x * 4.0
    y2 = y * y
    y4 = y2 * y2
    return (y4 * y4 * y2).astype(jnp.bfloat16)


def decode(code):
    return jnp.exp2(jnp.log2(code.astype(jnp.float32)) * 0.1) * 0.25


def pick(codes, value, count):
    out = jnp.full(codes.shape, value(0))
    for k in range(1, count):
        out = jnp.where(codes == k, value(k), out)
    return out


def right_kernel(out_hbm, tail_hbm, out_ref, code_ref, tail_ref, sems):
    size = out_ref.shape[0]
    step = size // CHUNKS
    parts = [pl.ds(k * step, step) for k in range(CHUNKS)]
    tails = [
        pltpu.make_async_copy(tail_hbm.at[part, :], tail_ref.at[part, :], sems.at[0, k])
        for k, part in enumerate(parts)
    ]
    outs = [
        pltpu.make_async_copy(out_hbm.at[part, :], out_ref.at[part, :], sems.at[1, k])
        for k, part in enumerate(parts)
    ]
    for copy in tails + outs:
        copy.start()
    for copy in tails:
        copy.wait()
    for part, copy in zip(parts, outs):
        copy.wait()
        term = lax.dot_general(
            out_ref[part, :],
            tail_ref[...],
            (((1,), (1,)), ((), ())),
            preferred_element_type=jnp.float32,
        )
        code_ref[part, :] = encode(term * (1.0 / size))


def left_kernel(flags_ref, head_ref, out_ref, after_ref, left_ref, code_ref):
    term = lax.dot_general(
        head_ref[...], out_ref[...], (((0,), (0,)), ((), ())), preferred_element_type=jnp.float32
    )
    term = jnp.where(flags_ref[0] == 1, term * (1.0 / term.shape[0]), 0.0)
    left_ref[...] = term
    code_ref[...] = encode(term)


def chip_kernel(flags_ref, left_ref, other_ref, right_ref, left_out_ref, code_ref):
    total = left_ref[...] + decode(other_ref[...])
    left_out_ref[...] = total

    @pl.when(flags_ref[1] == 1)
    def _():
        code_ref[...] = right_ref[...]

    @pl.when(flags_ref[1] == 0)
    def _():
        code_ref[...] = encode(total)


def add_kernel(a_ref, b_ref, code_ref):
    code_ref[...] = encode(decode(a_ref[...]) + decode(b_ref[...]))


def choose_kernel(flags_ref, a_ref, b_ref, after_ref, code_ref):
    @pl.when(flags_ref[2] == 1)
    def _():
        code_ref[...] = a_ref[...]

    @pl.when(flags_ref[2] == 0)
    def _():
        code_ref[...] = b_ref[...]


def masked_row(mask_ref, row, size):
    count = mask_ref.shape[1]
    place = lax.broadcasted_iota(jnp.int32, (1, size), 1) // (size // count)
    return pick(place, lambda k: mask_ref[row, k], count).astype(jnp.float32)


def column(row):
    return jnp.broadcast_to(row, (8, row.shape[1])).T[:, :1]


def factor_kernel(
    weight_ref, span_ref, partition_ref, head_ref, tail_ref, pair_ref, after_ref, factor_ref
):
    size = pair_ref.shape[0]
    kinds = weight_ref.shape[0]
    step = size // CHUNKS
    tail = tail_ref[...]
    head = column(head_ref[...].astype(jnp.float32)).astype(jnp.int32)
    table = [pick(tail, lambda k, j=j: weight_ref[j, k], kinds) for j in range(kinds)]
    reach = span_ref[0].astype(jnp.float32) * size
    for cell in range(CHUNKS):
        rows = pl.ds(cell * step, step)
        part = slice(cell * step, (cell + 1) * step)
        pairs = jnp.broadcast_to(table[0], (step, size))
        for j in range(1, kinds):
            pairs = jnp.where(head[part] == j, table[j], pairs)
        a = lax.broadcasted_iota(jnp.int32, (step, size), 0) + cell * step
        b = lax.broadcasted_iota(jnp.int32, (step, size), 1)
        span = reach + (b - a).astype(jnp.float32)
        penalty = jnp.sqrt(64.0 * size / span)
        factor_ref[rows, :] = pair_ref[rows, :] * pairs * penalty / partition_ref[0]


def partial_kernel(
    flags_ref,
    mask_ref,
    split_ref,
    head_ref,
    tail_ref,
    left_ref,
    middle_ref,
    first_ref,
    partial_ref,
    scale_ref,
):
    size = left_ref.shape[0]
    cells = mask_ref.shape[0]
    step = size // cells
    kinds = split_ref.shape[0]
    head = column(head_ref[...].astype(jnp.float32)).astype(jnp.int32)
    tail_weight = pick(tail_ref[...], lambda k: split_ref[k], kinds)
    head_weight = pick(head, lambda k: split_ref[k], kinds)
    for cell in range(cells):
        rows = pl.ds(cell * step, step)
        part = slice(cell * step, (cell + 1) * step)
        allowed = jnp.where(flags_ref[3] == 1, masked_row(mask_ref, cell, size), 0.0)
        right = decode(first_ref[rows, :]) * tail_weight
        left = (left_ref[rows, :] + decode(middle_ref[rows, :])) * head_weight[part]
        partial_ref[rows, :] = allowed * (right + left)
        scale_ref[pl.ds(cell, 1), :] = allowed * tail_weight


def last_kernel(
    scale_ref, partial_ref, factor_ref, inside_ref, last_ref, outside_ref, prob_ref
):
    cell = pl.program_id(0)
    step = outside_ref.shape[0]
    rows = pl.ds(cell * step, step)
    right = decode(inside_ref[rows, :]) + decode(last_ref[rows, :])
    total = partial_ref[rows, :] + scale_ref[pl.ds(cell, 1), :] * right
    outside_ref[...] = total
    prob_ref[...] = total * factor_ref[rows, :]


def routes(col_count):
    depth = col_count // 2

    def at(x, y, core, z):
        return (2 * y + core) * col_count + 2 * (z % depth) + x

    first, middle, last, inside = [], [], [], []
    for z in range(depth):
        o = z % 2
        n = 1 - o
        first += [(at(1, o, 0, z), at(0, o, 0, z)), (at(0, o, 0, z), at(0, o, 1, z))]
        first += [(at(0, o, 1, z), at(1, o, 0, z - 2)), (at(1, o, 1, z), at(1, o, 1, z - 2))]
        first += [(at(1, n, 0, z), at(0, n, 0, z)), (at(0, n, 1, z), at(1, n, 1, z))]
        first += [(at(0, n, 0, z), at(0, n, 1, z)), (at(1, n, 1, z), at(1, n, 0, z))]
        middle += [(at(0, o, 0, z), at(0, o, 1, z - 2)), (at(1, o, 1, z), at(1, o, 0, z))]
        for x in range(2):
            middle += [(at(x, n, x, z), at(x, o, x, z))]
            last += [(at(x, n, x, z), at(x, n, x, z - 1)), (at(x, o, x, z), at(x, o, 1 - x, z))]
            for pairs in (middle, last):
                pairs += [(at(x, o, 1 - x, z), at(x, n, 1 - x, z))]
                pairs += [(at(x, n, 1 - x, z), at(x, n, x, z))]
            for core in range(2):
                for side in range(2):
                    inside += [(at(x, side, core, z), at(x, side, 1 - core, z))]
    return first, middle, last, inside


def routed(
    outside,
    inside_head,
    inside_tail,
    inside_pair,
    seq_head,
    seq_tail,
    pair_mask,
    split_weight,
    pair_weight,
    span_blocks,
    partition,
):
    size = outside.shape[1]
    cells = pair_mask.shape[0]
    row_count = lax.axis_size("row")
    row_id = lax.axis_index("row")
    col_id = lax.axis_index("col")
    first, middle, last, inside = routes(lax.axis_size("col"))
    reach = (col_id - row_id) % row_count
    reach = jnp.where(reach == 0, row_count, reach)
    flags = jnp.stack(
        [
            col_id >= reach,
            row_id // 2 == (col_id // 2) % 2,
            col_id % 2 == 1,
            row_id == col_id % row_count,
        ]
    ).astype(jnp.int32)
    code = pltpu.VMEM((size, size), jnp.bfloat16)
    full = pltpu.VMEM((size, size), jnp.float32)
    output = jax.ShapeDtypeStruct((size, size), jnp.float32)

    def send(x, pairs):
        x = lax.ppermute(x, ("row", "col"), pairs)
        return pltpu.with_memory_space_constraint(x, pltpu.VMEM)

    def call(kernel, specs, shape, scratch=()):
        outs = tuple(VMEM for _ in shape) if isinstance(shape, tuple) else VMEM
        return pl.pallas_call(
            kernel,
            in_specs=specs,
            out_specs=outs,
            out_shape=shape,
            scratch_shapes=scratch,
            compiler_params=PARAMS,
        )

    held, right = call(
        right_kernel,
        [HBM] * 2,
        (code, code),
        [code, pltpu.SemaphoreType.DMA((2, CHUNKS))],
    )(
        pltpu.with_memory_space_constraint(outside, pltpu.HBM),
        pltpu.with_memory_space_constraint(inside_tail, pltpu.HBM),
    )
    q1 = send(right, first)
    left, left_code = call(left_kernel, [SMEM] + [VMEM] * 2 + [ANY], (full, code))(
        flags, inside_head, held, right
    )
    i0 = send(left_code, inside)
    left, moved = call(chip_kernel, [SMEM] + [VMEM] * 3, (full, code))(flags, left, i0, right)
    q3 = send(moved, middle)
    pair = call(add_kernel, [VMEM] * 2, code)(right, q1)
    q2 = send(pair, last)
    factor = call(factor_kernel, [SMEM] * 3 + [VMEM] * 3 + [ANY], full)(
        pair_weight, span_blocks, partition, seq_head, seq_tail, inside_pair, pair
    )
    chosen = call(choose_kernel, [SMEM] + [VMEM] * 2 + [ANY], code)(flags, q1, q3, factor)
    i2 = send(chosen, inside)
    partial, scale = call(
        partial_kernel,
        [SMEM] * 3 + [VMEM] * 5,
        (full, pltpu.VMEM((cells, size), jnp.float32)),
    )(flags, pair_mask, split_weight, seq_head, seq_tail, left, q3, q1)
    block = pl.BlockSpec((size // cells, size), lambda cell: (cell, 0))
    return pl.pallas_call(
        last_kernel,
        grid=(cells,),
        in_specs=[VMEM] * 5,
        out_specs=(block, block),
        out_shape=(output, output),
        compiler_params=PARAMS,
    )(scale, partial, factor, i2, q2)


def passed_along(x, axis, by):
    length = lax.axis_size(axis)
    return lax.ppermute(x, axis, [(i, (i + by) % length) for i in range(length)])


def finish(
    right_sum,
    left_sum,
    head_codes,
    tail_codes,
    mask_rows,
    pair_rows,
    split_weight,
    pair_weight,
    span_blocks,
    partition,
    owner_factor,
):
    cycles, tile_size = head_codes.shape
    repeat = tile_size // mask_rows.shape[1]
    allowed = jnp.repeat(
        jnp.repeat(mask_rows.astype(jnp.float32), repeat, axis=0), repeat, axis=1
    ).reshape(cycles, tile_size, tile_size)
    letters = jnp.arange(4, dtype=jnp.int32)
    head_hot = (head_codes[:, :, None] == letters[None, None, :]).astype(jnp.float32)
    tail_hot = (tail_codes[:, :, None] == letters[None, None, :]).astype(jnp.float32)
    head_weight = jnp.einsum("mak,k->ma", head_hot, split_weight, precision=precise)
    tail_weight = jnp.einsum("mak,k->ma", tail_hot, split_weight, precision=precise)
    outside_diag = (
        owner_factor
        * allowed
        * (right_sum * tail_weight[:, None, :] + head_weight[:, :, None] * left_sum)
        / tile_size
    )
    pair_table = jnp.einsum("mak,kl,mbl->mab", head_hot, pair_weight, tail_hot, precision=precise)
    positions = jnp.arange(tile_size, dtype=jnp.float32)
    span_nt = (
        tile_size * span_blocks[0].astype(jnp.float32) + positions[None, :] - positions[:, None]
    )
    penalty = jnp.sqrt(64.0 * tile_size / span_nt)
    pair_prob = (
        pair_rows.reshape(cycles, tile_size, tile_size)
        * outside_diag
        * pair_table
        * penalty[None, :, :]
        / partition[0]
    )
    return (
        outside_diag.reshape(cycles * tile_size, tile_size),
        pair_prob.reshape(cycles * tile_size, tile_size),
    )


def as_tiles(array):
    return array.reshape(-1, array.shape[1], array.shape[1])


def move_later(stack):
    return jnp.concatenate([jnp.zeros_like(stack), stack[:-1]], axis=0)


def general(
    outside,
    inside_head,
    inside_tail,
    inside_pair,
    seq_head,
    seq_tail,
    pair_mask,
    split_weight,
    pair_weight,
    span_blocks,
    partition,
):
    row_count = lax.axis_size("row")
    row_id = lax.axis_index("row")
    col_id = lax.axis_index("col")
    out_tiles = as_tiles(outside)
    right_part = jnp.einsum(
        "mac,mbc->mab", out_tiles, as_tiles(inside_tail), preferred_element_type=jnp.float32
    )
    window = passed_along(right_part, "col", -1)
    for level in range(row_count.bit_length() - 1):
        window = window + passed_along(window, "col", -(1 << level))
    reach = (col_id - row_id) % row_count
    reach = jnp.where(reach == 0, row_count, reach)
    left_part = jnp.einsum(
        "mca,mcb->mab", as_tiles(inside_head), out_tiles, preferred_element_type=jnp.float32
    )
    left_part = jnp.where(col_id < reach, move_later(left_part), left_part)
    left_sum = lax.psum(left_part, "row")
    owner_factor = (row_id == col_id % row_count).astype(jnp.float32)
    return finish(
        window,
        left_sum,
        seq_head,
        seq_tail,
        pair_mask,
        inside_pair,
        split_weight,
        pair_weight,
        span_blocks,
        partition,
        owner_factor,
    )


def per_device(use_routes, outside, *rest):
    return (routed if use_routes else general)(outside, *rest)


def solution(mesh):
    placed = (
        P("row", "col"),
        P("row", "col"),
        P("row", "col"),
        P(None, "col"),
        P(None, "col"),
        P(None, "col"),
        P(None, "col"),
        P(),
        P(),
        P(),
        P(),
    )

    def step(outside, *rest):
        rows, cols = mesh.shape["row"], mesh.shape["col"]
        one_tile = outside.shape[0] // rows == outside.shape[1] // cols
        use_routes = one_tile and rows == 4 and cols % 4 == 0
        body = jax.shard_map(
            lambda *args: per_device(use_routes, *args),
            mesh=mesh,
            in_specs=placed,
            out_specs=(P("row", "col"), P("row", "col")),
            check_vma=False,
        )
        return body(outside, *rest)

    return step
```

```python
import jax
import jax.numpy as jnp
from jax import lax
from jax.experimental import pallas as pl
from jax.experimental.pallas import tpu as pltpu
from jax.sharding import PartitionSpec as P


precise = lax.Precision.HIGHEST
VMEM = pl.BlockSpec(memory_space=pltpu.VMEM)
SMEM = pl.BlockSpec(memory_space=pltpu.SMEM)
ANY = pl.BlockSpec(memory_space=pl.ANY)
HBM = pl.BlockSpec(memory_space=pltpu.HBM)
CHUNKS = 4
PARAMS = pltpu.CompilerParams(vmem_limit_bytes=16 << 20)


def encode(x):
    y = x * 4.0
    y2 = y * y
    y4 = y2 * y2
    return (y4 * y4 * y2).astype(jnp.bfloat16)


def decode(code):
    return jnp.exp2(jnp.log2(code.astype(jnp.float32)) * 0.1) * 0.25


def pick(codes, value, count):
    out = jnp.full(codes.shape, value(0))
    for k in range(1, count):
        out = jnp.where(codes == k, value(k), out)
    return out


def right_kernel(out_hbm, tail_hbm, out_ref, code_ref, tail_ref, sems):
    tail = pltpu.make_async_copy(tail_hbm, tail_ref, sems.at[0])
    out = pltpu.make_async_copy(out_hbm, out_ref, sems.at[1])
    tail.start()
    out.start()
    tail.wait()
    out.wait()
    term = lax.dot_general(
        out_ref[...], tail_ref[...], (((1,), (1,)), ((), ())), preferred_element_type=jnp.float32
    )
    code_ref[...] = encode(term * (1.0 / term.shape[0]))


def left_kernel(flags_ref, head_ref, out_ref, after_ref, left_ref, code_ref):
    term = lax.dot_general(
        head_ref[...], out_ref[...], (((0,), (0,)), ((), ())), preferred_element_type=jnp.float32
    )
    term = jnp.where(flags_ref[0] == 1, term * (1.0 / term.shape[0]), 0.0)
    left_ref[...] = term
    code_ref[...] = encode(term)


def chip_kernel(flags_ref, left_ref, other_ref, right_ref, left_out_ref, code_ref):
    total = left_ref[...] + decode(other_ref[...])
    left_out_ref[...] = total

    @pl.when(flags_ref[1] == 1)
    def _():
        code_ref[...] = right_ref[...]

    @pl.when(flags_ref[1] == 0)
    def _():
        code_ref[...] = encode(total)


def add_kernel(a_ref, b_ref, code_ref):
    code_ref[...] = encode(decode(a_ref[...]) + decode(b_ref[...]))


def choose_kernel(flags_ref, a_ref, b_ref, after_ref, code_ref):
    @pl.when(flags_ref[2] == 1)
    def _():
        code_ref[...] = a_ref[...]

    @pl.when(flags_ref[2] == 0)
    def _():
        code_ref[...] = b_ref[...]


def masked_row(mask_ref, row, size):
    count = mask_ref.shape[1]
    place = lax.broadcasted_iota(jnp.int32, (1, size), 1) // (size // count)
    return pick(place, lambda k: mask_ref[row, k], count).astype(jnp.float32)


def column(row):
    return jnp.broadcast_to(row, (8, row.shape[1])).T[:, :1]


def factor_kernel(
    weight_ref, span_ref, partition_ref, head_ref, tail_ref, pair_ref, after_ref, factor_ref
):
    size = pair_ref.shape[0]
    kinds = weight_ref.shape[0]
    step = size // CHUNKS
    tail = tail_ref[...]
    head = column(head_ref[...].astype(jnp.float32)).astype(jnp.int32)
    table = [pick(tail, lambda k, j=j: weight_ref[j, k], kinds) for j in range(kinds)]
    reach = span_ref[0].astype(jnp.float32) * size
    for cell in range(CHUNKS):
        rows = pl.ds(cell * step, step)
        part = slice(cell * step, (cell + 1) * step)
        pairs = jnp.broadcast_to(table[0], (step, size))
        for j in range(1, kinds):
            pairs = jnp.where(head[part] == j, table[j], pairs)
        a = lax.broadcasted_iota(jnp.int32, (step, size), 0) + cell * step
        b = lax.broadcasted_iota(jnp.int32, (step, size), 1)
        span = reach + (b - a).astype(jnp.float32)
        penalty = jnp.sqrt(64.0 * size / span)
        factor_ref[rows, :] = pair_ref[rows, :] * pairs * penalty / partition_ref[0]


def partial_kernel(
    flags_ref,
    mask_ref,
    split_ref,
    head_ref,
    tail_ref,
    left_ref,
    middle_ref,
    first_ref,
    partial_ref,
    scale_ref,
):
    size = left_ref.shape[0]
    cells = mask_ref.shape[0]
    step = size // cells
    kinds = split_ref.shape[0]
    head = column(head_ref[...].astype(jnp.float32)).astype(jnp.int32)
    tail_weight = pick(tail_ref[...], lambda k: split_ref[k], kinds)
    head_weight = pick(head, lambda k: split_ref[k], kinds)
    for cell in range(cells):
        rows = pl.ds(cell * step, step)
        part = slice(cell * step, (cell + 1) * step)
        allowed = jnp.where(flags_ref[3] == 1, masked_row(mask_ref, cell, size), 0.0)
        right = decode(first_ref[rows, :]) * tail_weight
        left = (left_ref[rows, :] + decode(middle_ref[rows, :])) * head_weight[part]
        partial_ref[rows, :] = allowed * (right + left)
        scale_ref[pl.ds(cell, 1), :] = allowed * tail_weight


def last_kernel(
    scale_ref,
    partial_ref,
    factor_ref,
    inside_ref,
    last_ref,
    outside_hbm,
    prob_hbm,
    outside_ref,
    prob_ref,
    sems,
):
    cells = scale_ref.shape[0]
    step = outside_ref.shape[0] // cells
    copies = []
    for cell in range(cells):
        rows = pl.ds(cell * step, step)
        right = decode(inside_ref[rows, :]) + decode(last_ref[rows, :])
        total = partial_ref[rows, :] + scale_ref[pl.ds(cell, 1), :] * right
        outside_ref[rows, :] = total
        copies.append(
            pltpu.make_async_copy(
                outside_ref.at[rows, :], outside_hbm.at[rows, :], sems.at[0, cell]
            )
        )
        copies[-1].start()
        prob_ref[rows, :] = total * factor_ref[rows, :]
        copies.append(
            pltpu.make_async_copy(prob_ref.at[rows, :], prob_hbm.at[rows, :], sems.at[1, cell])
        )
        copies[-1].start()
    for copy in copies:
        copy.wait()


def routes(col_count):
    depth = col_count // 2

    def at(x, y, core, z):
        return (2 * y + core) * col_count + 2 * (z % depth) + x

    first, middle, last, inside = [], [], [], []
    for z in range(depth):
        o = z % 2
        n = 1 - o
        first += [(at(1, o, 0, z), at(0, o, 0, z)), (at(0, o, 0, z), at(0, o, 1, z))]
        first += [(at(0, o, 1, z), at(1, o, 0, z - 2)), (at(1, o, 1, z), at(1, o, 1, z - 2))]
        first += [(at(1, n, 0, z), at(0, n, 0, z)), (at(0, n, 1, z), at(1, n, 1, z))]
        first += [(at(0, n, 0, z), at(0, n, 1, z)), (at(1, n, 1, z), at(1, n, 0, z))]
        middle += [(at(0, o, 0, z), at(0, o, 1, z - 2)), (at(1, o, 1, z), at(1, o, 0, z))]
        for x in range(2):
            middle += [(at(x, n, x, z), at(x, o, x, z))]
            last += [(at(x, n, x, z), at(x, n, x, z - 1)), (at(x, o, x, z), at(x, o, 1 - x, z))]
            for pairs in (middle, last):
                pairs += [(at(x, o, 1 - x, z), at(x, n, 1 - x, z))]
                pairs += [(at(x, n, 1 - x, z), at(x, n, x, z))]
            for core in range(2):
                for side in range(2):
                    inside += [(at(x, side, core, z), at(x, side, 1 - core, z))]
    return first, middle, last, inside


def routed(
    outside,
    inside_head,
    inside_tail,
    inside_pair,
    seq_head,
    seq_tail,
    pair_mask,
    split_weight,
    pair_weight,
    span_blocks,
    partition,
):
    size = outside.shape[1]
    cells = pair_mask.shape[0]
    row_count = lax.axis_size("row")
    row_id = lax.axis_index("row")
    col_id = lax.axis_index("col")
    first, middle, last, inside = routes(lax.axis_size("col"))
    reach = (col_id - row_id) % row_count
    reach = jnp.where(reach == 0, row_count, reach)
    flags = jnp.stack(
        [
            col_id >= reach,
            row_id // 2 == (col_id // 2) % 2,
            col_id % 2 == 1,
            row_id == col_id % row_count,
        ]
    ).astype(jnp.int32)
    code = pltpu.VMEM((size, size), jnp.bfloat16)
    full = pltpu.VMEM((size, size), jnp.float32)
    output = pltpu.HBM((size, size), jnp.float32)

    def send(x, pairs):
        x = lax.ppermute(x, ("row", "col"), pairs)
        return pltpu.with_memory_space_constraint(x, pltpu.VMEM)

    def call(kernel, specs, shape, scratch=()):
        outs = tuple(VMEM for _ in shape) if isinstance(shape, tuple) else VMEM
        return pl.pallas_call(
            kernel,
            in_specs=specs,
            out_specs=outs,
            out_shape=shape,
            scratch_shapes=scratch,
            compiler_params=PARAMS,
        )

    held, right = call(
        right_kernel,
        [HBM] * 2,
        (code, code),
        [code, pltpu.SemaphoreType.DMA((2,))],
    )(
        pltpu.with_memory_space_constraint(outside, pltpu.HBM),
        pltpu.with_memory_space_constraint(inside_tail, pltpu.HBM),
    )
    q1 = send(right, first)
    left, left_code = call(left_kernel, [SMEM] + [VMEM] * 2 + [ANY], (full, code))(
        flags, inside_head, held, right
    )
    i0 = send(left_code, inside)
    left, moved = call(chip_kernel, [SMEM] + [VMEM] * 3, (full, code))(flags, left, i0, right)
    q3 = send(moved, middle)
    pair = call(add_kernel, [VMEM] * 2, code)(right, q1)
    q2 = send(pair, last)
    factor = call(factor_kernel, [SMEM] * 3 + [VMEM] * 3 + [ANY], full)(
        pair_weight, span_blocks, partition, seq_head, seq_tail, inside_pair, pair
    )
    chosen = call(choose_kernel, [SMEM] + [VMEM] * 2 + [ANY], code)(flags, q1, q3, factor)
    i2 = send(chosen, inside)
    partial, scale = call(
        partial_kernel,
        [SMEM] * 3 + [VMEM] * 5,
        (full, pltpu.VMEM((cells, size), jnp.float32)),
    )(flags, pair_mask, split_weight, seq_head, seq_tail, left, q3, q1)
    return pl.pallas_call(
        last_kernel,
        in_specs=[VMEM] * 5,
        out_specs=(HBM, HBM),
        out_shape=(output, output),
        scratch_shapes=[full, full, pltpu.SemaphoreType.DMA((2, cells))],
        compiler_params=PARAMS,
    )(scale, partial, factor, i2, q2)


def passed_along(x, axis, by):
    length = lax.axis_size(axis)
    return lax.ppermute(x, axis, [(i, (i + by) % length) for i in range(length)])


def finish(
    right_sum,
    left_sum,
    head_codes,
    tail_codes,
    mask_rows,
    pair_rows,
    split_weight,
    pair_weight,
    span_blocks,
    partition,
    owner_factor,
):
    cycles, tile_size = head_codes.shape
    repeat = tile_size // mask_rows.shape[1]
    allowed = jnp.repeat(
        jnp.repeat(mask_rows.astype(jnp.float32), repeat, axis=0), repeat, axis=1
    ).reshape(cycles, tile_size, tile_size)
    letters = jnp.arange(4, dtype=jnp.int32)
    head_hot = (head_codes[:, :, None] == letters[None, None, :]).astype(jnp.float32)
    tail_hot = (tail_codes[:, :, None] == letters[None, None, :]).astype(jnp.float32)
    head_weight = jnp.einsum("mak,k->ma", head_hot, split_weight, precision=precise)
    tail_weight = jnp.einsum("mak,k->ma", tail_hot, split_weight, precision=precise)
    outside_diag = (
        owner_factor
        * allowed
        * (right_sum * tail_weight[:, None, :] + head_weight[:, :, None] * left_sum)
        / tile_size
    )
    pair_table = jnp.einsum("mak,kl,mbl->mab", head_hot, pair_weight, tail_hot, precision=precise)
    positions = jnp.arange(tile_size, dtype=jnp.float32)
    span_nt = (
        tile_size * span_blocks[0].astype(jnp.float32) + positions[None, :] - positions[:, None]
    )
    penalty = jnp.sqrt(64.0 * tile_size / span_nt)
    pair_prob = (
        pair_rows.reshape(cycles, tile_size, tile_size)
        * outside_diag
        * pair_table
        * penalty[None, :, :]
        / partition[0]
    )
    return (
        outside_diag.reshape(cycles * tile_size, tile_size),
        pair_prob.reshape(cycles * tile_size, tile_size),
    )


def as_tiles(array):
    return array.reshape(-1, array.shape[1], array.shape[1])


def move_later(stack):
    return jnp.concatenate([jnp.zeros_like(stack), stack[:-1]], axis=0)


def general(
    outside,
    inside_head,
    inside_tail,
    inside_pair,
    seq_head,
    seq_tail,
    pair_mask,
    split_weight,
    pair_weight,
    span_blocks,
    partition,
):
    row_count = lax.axis_size("row")
    row_id = lax.axis_index("row")
    col_id = lax.axis_index("col")
    out_tiles = as_tiles(outside)
    right_part = jnp.einsum(
        "mac,mbc->mab", out_tiles, as_tiles(inside_tail), preferred_element_type=jnp.float32
    )
    window = passed_along(right_part, "col", -1)
    for level in range(row_count.bit_length() - 1):
        window = window + passed_along(window, "col", -(1 << level))
    reach = (col_id - row_id) % row_count
    reach = jnp.where(reach == 0, row_count, reach)
    left_part = jnp.einsum(
        "mca,mcb->mab", as_tiles(inside_head), out_tiles, preferred_element_type=jnp.float32
    )
    left_part = jnp.where(col_id < reach, move_later(left_part), left_part)
    left_sum = lax.psum(left_part, "row")
    owner_factor = (row_id == col_id % row_count).astype(jnp.float32)
    return finish(
        window,
        left_sum,
        seq_head,
        seq_tail,
        pair_mask,
        inside_pair,
        split_weight,
        pair_weight,
        span_blocks,
        partition,
        owner_factor,
    )


def per_device(use_routes, outside, *rest):
    return (routed if use_routes else general)(outside, *rest)


def solution(mesh):
    placed = (
        P("row", "col"),
        P("row", "col"),
        P("row", "col"),
        P(None, "col"),
        P(None, "col"),
        P(None, "col"),
        P(None, "col"),
        P(),
        P(),
        P(),
        P(),
    )

    def step(outside, *rest):
        rows, cols = mesh.shape["row"], mesh.shape["col"]
        one_tile = outside.shape[0] // rows == outside.shape[1] // cols
        use_routes = one_tile and rows == 4 and cols % 4 == 0
        body = jax.shard_map(
            lambda *args: per_device(use_routes, *args),
            mesh=mesh,
            in_specs=placed,
            out_specs=(P("row", "col"), P("row", "col")),
            check_vma=False,
        )
        return body(outside, *rest)

    return step
```

```python
import jax
import jax.numpy as jnp
from jax import lax
from jax.experimental import pallas as pl
from jax.experimental.pallas import tpu as pltpu
from jax.sharding import PartitionSpec as P


precise = lax.Precision.HIGHEST
VMEM = pl.BlockSpec(memory_space=pltpu.VMEM)
SMEM = pl.BlockSpec(memory_space=pltpu.SMEM)
ANY = pl.BlockSpec(memory_space=pl.ANY)
HBM = pl.BlockSpec(memory_space=pltpu.HBM)
CHUNKS = 4
PARAMS = pltpu.CompilerParams(vmem_limit_bytes=16 << 20)


def encode(x):
    y = x * 4.0
    y2 = y * y
    y4 = y2 * y2
    return (y4 * y4 * y2).astype(jnp.bfloat16)


def decode(code):
    return jnp.exp2(jnp.log2(code.astype(jnp.float32)) * 0.1) * 0.25


def pick(codes, value, count):
    out = jnp.full(codes.shape, value(0))
    for k in range(1, count):
        out = jnp.where(codes == k, value(k), out)
    return out


def right_kernel(out_hbm, tail_hbm, out_ref, code_ref, rest_ref, tail_ref, sems):
    tail = pltpu.make_async_copy(tail_hbm, tail_ref, sems.at[0])
    out = pltpu.make_async_copy(out_hbm, out_ref, sems.at[1])
    tail.start()
    out.start()
    tail.wait()
    out.wait()
    term = lax.dot_general(
        out_ref[...], tail_ref[...], (((1,), (1,)), ((), ())), preferred_element_type=jnp.float32
    )
    code_ref[...] = encode(term * (1.0 / term.shape[0]))
    half = rest_ref.shape[0]
    rest_ref[...] = code_ref[pl.ds(half, half), :]


def left_kernel(flags_ref, head_ref, out_ref, after_ref, left_ref, code_ref):
    term = lax.dot_general(
        head_ref[...], out_ref[...], (((0,), (0,)), ((), ())), preferred_element_type=jnp.float32
    )
    term = jnp.where(flags_ref[0] == 1, term * (1.0 / term.shape[0]), 0.0)
    left_ref[...] = term
    code_ref[...] = encode(term)


def relay_kernel(flags_ref, right_ref, across_ref, after_ref, code_ref):
    @pl.when(flags_ref[2] == 1)
    def _():
        code_ref[...] = across_ref[...]

    @pl.when(flags_ref[2] == 0)
    def _():
        code_ref[...] = right_ref[pl.ds(0, code_ref.shape[0]), :]


def chip_kernel(left_ref, other_ref, left_out_ref, code_ref):
    total = left_ref[...] + decode(other_ref[...])
    left_out_ref[...] = total
    code_ref[...] = encode(total)


def add_kernel(a_ref, b_ref, code_ref):
    code_ref[...] = encode(decode(a_ref[...]) + decode(b_ref[...]))


def masked_row(mask_ref, row, size):
    count = mask_ref.shape[1]
    place = lax.broadcasted_iota(jnp.int32, (1, size), 1) // (size // count)
    return pick(place, lambda k: mask_ref[row, k], count).astype(jnp.float32)


def column(row):
    return jnp.broadcast_to(row, (8, row.shape[1])).T[:, :1]


def factor_kernel(
    weight_ref,
    head_ref,
    tail_ref,
    pair_ref,
    span_hbm,
    partition_hbm,
    after_ref,
    factor_ref,
    span_ref,
    partition_ref,
    sems,
):
    scalars = [
        pltpu.make_async_copy(span_hbm, span_ref, sems.at[0]),
        pltpu.make_async_copy(partition_hbm, partition_ref, sems.at[1]),
    ]
    for copy in scalars:
        copy.start()
    for copy in scalars:
        copy.wait()
    size = pair_ref.shape[0]
    kinds = weight_ref.shape[0]
    step = size // CHUNKS
    tail = tail_ref[...]
    head = column(head_ref[...].astype(jnp.float32)).astype(jnp.int32)
    table = [pick(tail, lambda k, j=j: weight_ref[j, k], kinds) for j in range(kinds)]
    reach = span_ref[0].astype(jnp.float32) * size
    for cell in range(CHUNKS):
        rows = pl.ds(cell * step, step)
        part = slice(cell * step, (cell + 1) * step)
        pairs = jnp.broadcast_to(table[0], (step, size))
        for j in range(1, kinds):
            pairs = jnp.where(head[part] == j, table[j], pairs)
        a = lax.broadcasted_iota(jnp.int32, (step, size), 0) + cell * step
        b = lax.broadcasted_iota(jnp.int32, (step, size), 1)
        span = reach + (b - a).astype(jnp.float32)
        penalty = jnp.sqrt(64.0 * size / span)
        factor_ref[rows, :] = pair_ref[rows, :] * pairs * penalty / partition_ref[0]


def partial_kernel(
    flags_ref,
    mask_ref,
    split_ref,
    head_ref,
    tail_ref,
    left_ref,
    middle_ref,
    first_ref,
    across_ref,
    far_ref,
    inside_ref,
    partial_ref,
    scale_ref,
):
    size = left_ref.shape[0]
    cells = mask_ref.shape[0]
    step = size // cells
    kinds = split_ref.shape[0]
    head = column(head_ref[...].astype(jnp.float32)).astype(jnp.int32)
    tail_weight = pick(tail_ref[...], lambda k: split_ref[k], kinds)
    head_weight = pick(head, lambda k: split_ref[k], kinds)
    for cell in range(cells):
        rows = pl.ds(cell * step, step)
        part = slice(cell * step, (cell + 1) * step)
        rest = pl.ds(cell * step % far_ref.shape[0], step)
        even, odd = (far_ref, inside_ref) if 2 * cell < cells else (across_ref, far_ref)
        code = jnp.where(
            flags_ref[1] == 1,
            odd[rest, :].astype(jnp.float32),
            even[rest, :].astype(jnp.float32),
        )
        allowed = jnp.where(flags_ref[3] == 1, masked_row(mask_ref, cell, size), 0.0)
        right = (decode(first_ref[rows, :]) + decode(code)) * tail_weight
        left = (left_ref[rows, :] + decode(middle_ref[rows, :])) * head_weight[part]
        partial_ref[rows, :] = allowed * (right + left)
        scale_ref[pl.ds(cell, 1), :] = allowed * tail_weight


def last_kernel(
    scale_ref,
    partial_ref,
    factor_ref,
    last_ref,
    outside_hbm,
    prob_hbm,
    outside_ref,
    prob_ref,
    sems,
):
    cells = scale_ref.shape[0]
    step = outside_ref.shape[0] // cells
    copies = []
    for cell in range(cells):
        rows = pl.ds(cell * step, step)
        total = partial_ref[rows, :] + scale_ref[pl.ds(cell, 1), :] * decode(last_ref[rows, :])
        outside_ref[rows, :] = total
        copies.append(
            pltpu.make_async_copy(
                outside_ref.at[rows, :], outside_hbm.at[rows, :], sems.at[0, cell]
            )
        )
        copies[-1].start()
        prob_ref[rows, :] = total * factor_ref[rows, :]
        copies.append(
            pltpu.make_async_copy(prob_ref.at[rows, :], prob_hbm.at[rows, :], sems.at[1, cell])
        )
        copies[-1].start()
    for copy in copies:
        copy.wait()


def routes(col_count):
    depth = col_count // 2

    def at(x, y, core, z):
        return (2 * y + core) * col_count + 2 * (z % depth) + x

    first, across, far, middle, last, inside = [], [], [], [], [], []
    for z in range(depth):
        o = z % 2
        n = 1 - o
        for x in range(2):
            mine, other = at(x, o, x, z), at(x, o, 1 - x, z)
            near, spare = at(x, n, x, z), at(x, n, 1 - x, z)
            first += [(mine, at(x, o, x, z - 2)), (spare, at(1 - x, n, 1 - x, z))]
            first += [(near, other), (other, spare)]
            across += [(other, at(1 - x, o, 1 - x, z)), (mine, other)]
            middle += [(near, mine), (mine, other), (other, spare), (spare, near)]
            last += [(near, at(x, n, x, z - 1)), (mine, other), (spare, near)]
            last += [(other, at(x, o, 1 - x, z ^ 1))]
            for side in range(2):
                inside += [(at(x, side, core, z), at(x, side, 1 - core, z)) for core in range(2)]
            for pairs in (across, far):
                pairs += [(near, spare), (spare, near)]
        far += [(at(1, o, 0, z), at(0, o, 0, z)), (at(0, o, 0, z), at(0, o, 1, z))]
        far += [(at(0, o, 1, z), at(1, o, 0, z - 2)), (at(1, o, 1, z), at(1, o, 1, z - 2))]
    return first, across, far, middle, last, inside


def routed(
    outside,
    inside_head,
    inside_tail,
    inside_pair,
    seq_head,
    seq_tail,
    pair_mask,
    split_weight,
    pair_weight,
    span_blocks,
    partition,
):
    size = outside.shape[1]
    cells = pair_mask.shape[0]
    row_count = lax.axis_size("row")
    row_id = lax.axis_index("row")
    col_id = lax.axis_index("col")
    first, across, far, middle, last, inside = routes(lax.axis_size("col"))
    reach = (col_id - row_id) % row_count
    reach = jnp.where(reach == 0, row_count, reach)
    flags = [
        col_id >= reach,
        col_id % 2 == 1,
        (col_id % 2) * (row_id % 2) == 1,
        row_id == col_id % row_count,
    ]
    flags = jnp.stack(flags).astype(jnp.int32)
    code = pltpu.VMEM((size, size), jnp.bfloat16)
    full = pltpu.VMEM((size, size), jnp.float32)
    output = pltpu.HBM((size, size), jnp.float32)

    def send(x, pairs):
        x = lax.ppermute(x, ("row", "col"), pairs)
        return pltpu.with_memory_space_constraint(x, pltpu.VMEM)

    def call(kernel, specs, shape, scratch=()):
        outs = tuple(VMEM for _ in shape) if isinstance(shape, tuple) else VMEM
        return pl.pallas_call(
            kernel,
            in_specs=specs,
            out_specs=outs,
            out_shape=shape,
            scratch_shapes=scratch,
            compiler_params=PARAMS,
        )

    half = pltpu.VMEM((size // 2, size), jnp.bfloat16)
    held, right, rest = call(
        right_kernel,
        [HBM] * 2,
        (code, code, half),
        [code, pltpu.SemaphoreType.DMA((2,))],
    )(
        pltpu.with_memory_space_constraint(outside, pltpu.HBM),
        pltpu.with_memory_space_constraint(inside_tail, pltpu.HBM),
    )
    q1 = send(right, first)
    qx = send(rest, across)
    left, left_code = call(left_kernel, [SMEM] + [VMEM] * 2 + [ANY], (full, code))(
        flags, inside_head, held, right
    )
    i0 = send(left_code, inside)
    left, moved = call(chip_kernel, [VMEM] * 2, (full, code))(left, i0)
    q4 = send(moved, middle)
    relayed = call(relay_kernel, [SMEM] + [VMEM] * 2 + [ANY], half)(
        flags, right, qx, moved
    )
    q3 = send(relayed, far)
    pair = call(add_kernel, [VMEM] * 2, code)(right, q1)
    q2 = send(pair, last)
    factor = call(
        factor_kernel,
        [SMEM] + [VMEM] * 3 + [ANY] * 3,
        full,
        [pltpu.SMEM((1,), jnp.int32), pltpu.SMEM((1,), jnp.float32), pltpu.SemaphoreType.DMA((2,))],
    )(pair_weight, seq_head, seq_tail, inside_pair, span_blocks, partition, pair)
    i2 = send(q3, inside)
    partial, scale = call(
        partial_kernel,
        [SMEM] * 3 + [VMEM] * 8,
        (full, pltpu.VMEM((cells, size), jnp.float32)),
    )(
        flags,
        pair_mask,
        split_weight,
        seq_head,
        seq_tail,
        left,
        q4,
        q1,
        qx,
        q3,
        i2,
    )
    return pl.pallas_call(
        last_kernel,
        in_specs=[VMEM] * 4,
        out_specs=(HBM, HBM),
        out_shape=(output, output),
        scratch_shapes=[full, full, pltpu.SemaphoreType.DMA((2, cells))],
        compiler_params=PARAMS,
    )(scale, partial, factor, q2)


def passed_along(x, axis, by):
    length = lax.axis_size(axis)
    return lax.ppermute(x, axis, [(i, (i + by) % length) for i in range(length)])


def finish(
    right_sum,
    left_sum,
    head_codes,
    tail_codes,
    mask_rows,
    pair_rows,
    split_weight,
    pair_weight,
    span_blocks,
    partition,
    owner_factor,
):
    cycles, tile_size = head_codes.shape
    repeat = tile_size // mask_rows.shape[1]
    allowed = jnp.repeat(
        jnp.repeat(mask_rows.astype(jnp.float32), repeat, axis=0), repeat, axis=1
    ).reshape(cycles, tile_size, tile_size)
    letters = jnp.arange(4, dtype=jnp.int32)
    head_hot = (head_codes[:, :, None] == letters[None, None, :]).astype(jnp.float32)
    tail_hot = (tail_codes[:, :, None] == letters[None, None, :]).astype(jnp.float32)
    head_weight = jnp.einsum("mak,k->ma", head_hot, split_weight, precision=precise)
    tail_weight = jnp.einsum("mak,k->ma", tail_hot, split_weight, precision=precise)
    outside_diag = (
        owner_factor
        * allowed
        * (right_sum * tail_weight[:, None, :] + head_weight[:, :, None] * left_sum)
        / tile_size
    )
    pair_table = jnp.einsum("mak,kl,mbl->mab", head_hot, pair_weight, tail_hot, precision=precise)
    positions = jnp.arange(tile_size, dtype=jnp.float32)
    span_nt = (
        tile_size * span_blocks[0].astype(jnp.float32) + positions[None, :] - positions[:, None]
    )
    penalty = jnp.sqrt(64.0 * tile_size / span_nt)
    pair_prob = (
        pair_rows.reshape(cycles, tile_size, tile_size)
        * outside_diag
        * pair_table
        * penalty[None, :, :]
        / partition[0]
    )
    return (
        outside_diag.reshape(cycles * tile_size, tile_size),
        pair_prob.reshape(cycles * tile_size, tile_size),
    )


def as_tiles(array):
    return array.reshape(-1, array.shape[1], array.shape[1])


def move_later(stack):
    return jnp.concatenate([jnp.zeros_like(stack), stack[:-1]], axis=0)


def general(
    outside,
    inside_head,
    inside_tail,
    inside_pair,
    seq_head,
    seq_tail,
    pair_mask,
    split_weight,
    pair_weight,
    span_blocks,
    partition,
):
    row_count = lax.axis_size("row")
    row_id = lax.axis_index("row")
    col_id = lax.axis_index("col")
    out_tiles = as_tiles(outside)
    right_part = jnp.einsum(
        "mac,mbc->mab", out_tiles, as_tiles(inside_tail), preferred_element_type=jnp.float32
    )
    window = passed_along(right_part, "col", -1)
    for level in range(row_count.bit_length() - 1):
        window = window + passed_along(window, "col", -(1 << level))
    reach = (col_id - row_id) % row_count
    reach = jnp.where(reach == 0, row_count, reach)
    left_part = jnp.einsum(
        "mca,mcb->mab", as_tiles(inside_head), out_tiles, preferred_element_type=jnp.float32
    )
    left_part = jnp.where(col_id < reach, move_later(left_part), left_part)
    left_sum = lax.psum(left_part, "row")
    owner_factor = (row_id == col_id % row_count).astype(jnp.float32)
    return finish(
        window,
        left_sum,
        seq_head,
        seq_tail,
        pair_mask,
        inside_pair,
        split_weight,
        pair_weight,
        span_blocks,
        partition,
        owner_factor,
    )


def per_device(use_routes, outside, *rest):
    return (routed if use_routes else general)(outside, *rest)


def solution(mesh):
    placed = (
        P("row", "col"),
        P("row", "col"),
        P("row", "col"),
        P(None, "col"),
        P(None, "col"),
        P(None, "col"),
        P(None, "col"),
        P(),
        P(),
        P(),
        P(),
    )

    def step(outside, *rest):
        rows, cols = mesh.shape["row"], mesh.shape["col"]
        one_tile = outside.shape[0] // rows == outside.shape[1] // cols
        use_routes = one_tile and rows == 4 and cols % 4 == 0
        body = jax.shard_map(
            lambda *args: per_device(use_routes, *args),
            mesh=mesh,
            in_specs=placed,
            out_specs=(P("row", "col"), P("row", "col")),
            check_vma=False,
        )
        return body(outside, *rest)

    return step
```

```python
import functools

import jax
import jax.numpy as jnp
from jax import lax
from jax.experimental import pallas as pl
from jax.experimental.pallas import tpu as pltpu
from jax.sharding import PartitionSpec as P


precise = lax.Precision.HIGHEST
VMEM = pl.BlockSpec(memory_space=pltpu.VMEM)
SMEM = pl.BlockSpec(memory_space=pltpu.SMEM)
ANY = pl.BlockSpec(memory_space=pl.ANY)
HBM = pl.BlockSpec(memory_space=pltpu.HBM)
CHUNKS = 4
PARAMS = pltpu.CompilerParams(vmem_limit_bytes=16 << 20)


def encode(x):
    y = x * 4.0
    y2 = y * y
    y4 = y2 * y2
    return (y4 * y4 * y2).astype(jnp.bfloat16)


def decode(code):
    return jnp.exp2(jnp.log2(code.astype(jnp.float32)) * 0.1) * 0.25


def place():
    return lax.axis_index("row"), lax.axis_index("col")


def pick(codes, value, count):
    out = jnp.full(codes.shape, value(0))
    for k in range(1, count):
        out = jnp.where(codes == k, value(k), out)
    return out


def right_kernel(out_hbm, tail_hbm, out_ref, code_ref, top_ref, rest_ref, tail_ref, sems):
    tail = pltpu.make_async_copy(tail_hbm, tail_ref, sems.at[0])
    out = pltpu.make_async_copy(out_hbm, out_ref, sems.at[1])
    tail.start()
    out.start()
    tail.wait()
    out.wait()
    term = lax.dot_general(
        out_ref[...], tail_ref[...], (((1,), (1,)), ((), ())), preferred_element_type=jnp.float32
    )
    code_ref[...] = encode(term * (1.0 / term.shape[0]))
    half = rest_ref.shape[0]
    top_ref[...] = code_ref[pl.ds(0, half), :]
    rest_ref[...] = code_ref[pl.ds(half, half), :]


def left_kernel(rows, head_ref, out_ref, after_ref, left_ref, code_ref):
    term = lax.dot_general(
        head_ref[...], out_ref[...], (((0,), (0,)), ((), ())), preferred_element_type=jnp.float32
    )
    row_id, col_id = place()
    reach = lax.rem(col_id - row_id + 2 * rows, rows)
    reach = jnp.where(reach == 0, rows, reach)
    term = jnp.where(col_id >= reach, term * (1.0 / term.shape[0]), 0.0)
    left_ref[...] = term
    code_ref[...] = encode(term)


def chip_kernel(left_ref, other_ref, left_out_ref, code_ref):
    total = left_ref[...] + decode(other_ref[...])
    left_out_ref[...] = total
    code_ref[...] = encode(total)


def add_kernel(a_ref, b_ref, code_ref):
    code_ref[...] = encode(decode(a_ref[...]) + decode(b_ref[...]))


def masked_row(mask_ref, row, size):
    count = mask_ref.shape[1]
    place = lax.broadcasted_iota(jnp.int32, (1, size), 1) // (size // count)
    return pick(place, lambda k: mask_ref[row, k], count).astype(jnp.float32)


def column(row):
    return jnp.broadcast_to(row, (8, row.shape[1])).T[:, :1]


def factor_kernel(
    weight_ref,
    head_ref,
    tail_ref,
    pair_ref,
    span_hbm,
    partition_hbm,
    after_ref,
    factor_ref,
    span_ref,
    partition_ref,
    sems,
):
    scalars = [
        pltpu.make_async_copy(span_hbm, span_ref, sems.at[0]),
        pltpu.make_async_copy(partition_hbm, partition_ref, sems.at[1]),
    ]
    for copy in scalars:
        copy.start()
    for copy in scalars:
        copy.wait()
    size = pair_ref.shape[0]
    kinds = weight_ref.shape[0]
    step = size // CHUNKS
    tail = tail_ref[...]
    head = column(head_ref[...].astype(jnp.float32)).astype(jnp.int32)
    table = [pick(tail, lambda k, j=j: weight_ref[j, k], kinds) for j in range(kinds)]
    reach = span_ref[0].astype(jnp.float32) * size
    for cell in range(CHUNKS):
        rows = pl.ds(cell * step, step)
        part = slice(cell * step, (cell + 1) * step)
        pairs = jnp.broadcast_to(table[0], (step, size))
        for j in range(1, kinds):
            pairs = jnp.where(head[part] == j, table[j], pairs)
        a = lax.broadcasted_iota(jnp.int32, (step, size), 0) + cell * step
        b = lax.broadcasted_iota(jnp.int32, (step, size), 1)
        span = reach + (b - a).astype(jnp.float32)
        penalty = jnp.sqrt(64.0 * size / span)
        factor_ref[rows, :] = pair_ref[rows, :] * pairs * penalty / partition_ref[0]


def partial_kernel(
    rows_count,
    mask_ref,
    split_ref,
    head_ref,
    tail_ref,
    left_ref,
    middle_ref,
    far_ref,
    across_ref,
    direct_ref,
    partial_ref,
    scale_ref,
):
    size = left_ref.shape[0]
    cells = mask_ref.shape[0]
    step = size // cells
    kinds = split_ref.shape[0]
    row_id, col_id = place()
    is_owner = row_id == lax.rem(col_id, rows_count)
    head = column(head_ref[...].astype(jnp.float32)).astype(jnp.int32)
    tail_weight = pick(tail_ref[...], lambda k: split_ref[k], kinds)
    head_weight = pick(head, lambda k: split_ref[k], kinds)
    for cell in range(cells):
        rows = pl.ds(cell * step, step)
        part = slice(cell * step, (cell + 1) * step)
        if 2 * cell < cells:
            code = direct_ref[rows, :].astype(jnp.float32)
        else:
            code = across_ref[pl.ds((cell - cells // 2) * step, step), :].astype(jnp.float32)
            code = jnp.where(lax.rem(col_id, 2) == 0, code, 0.0)
        allowed = jnp.where(is_owner, masked_row(mask_ref, cell, size), 0.0)
        right = (decode(far_ref[rows, :]) + decode(code)) * tail_weight
        left = (left_ref[rows, :] + decode(middle_ref[rows, :])) * head_weight[part]
        partial_ref[rows, :] = allowed * (right + left)
        scale_ref[pl.ds(cell, 1), :] = allowed * tail_weight


def last_kernel(
    scale_ref,
    partial_ref,
    factor_ref,
    relay_ref,
    last_ref,
    outside_hbm,
    prob_hbm,
    outside_ref,
    prob_ref,
    sems,
):
    _, col_id = place()
    cells = scale_ref.shape[0]
    step = outside_ref.shape[0] // cells
    copies = []
    for cell in range(cells):
        rows = pl.ds(cell * step, step)
        right = decode(last_ref[rows, :])
        if 2 * cell >= cells:
            code = relay_ref[pl.ds((cell - cells // 2) * step, step), :].astype(jnp.float32)
            right += decode(jnp.where(lax.rem(col_id, 2) == 1, code, 0.0))
        total = partial_ref[rows, :] + scale_ref[pl.ds(cell, 1), :] * right
        outside_ref[rows, :] = total
        copies.append(
            pltpu.make_async_copy(
                outside_ref.at[rows, :], outside_hbm.at[rows, :], sems.at[0, cell]
            )
        )
        copies[-1].start()
        prob_ref[rows, :] = total * factor_ref[rows, :]
        copies.append(
            pltpu.make_async_copy(prob_ref.at[rows, :], prob_hbm.at[rows, :], sems.at[1, cell])
        )
        copies[-1].start()
    for copy in copies:
        copy.wait()


def routes(col_count):
    depth = col_count // 2

    def at(x, y, core, z):
        return (2 * y + core) * col_count + 2 * (z % depth) + x

    first, across, far, direct, middle, relay, last, inside = [[] for _ in range(8)]
    for z in range(depth):
        o = z % 2
        n = 1 - o
        for x in range(2):
            mine, other = at(x, o, x, z), at(x, o, 1 - x, z)
            near, spare = at(x, n, x, z), at(x, n, 1 - x, z)
            first += [(mine, other), (other, mine)]
            first += [(spare, at(1 - x, n, 1 - x, z)), (near, spare)]
            across += [(other, at(1 - x, o, 1 - x, z)), (mine, other)]
            far += [(mine, at(x, o, x, z - 2)), (other, spare), (spare, near), (near, other)]
            direct += [(other, at(1 - x, o, 1 - x, z + 2 * x - 2)), (mine, other)]
            middle += [(near, mine), (mine, other), (other, spare), (spare, near)]
            last += [(near, at(x, n, x, z - 1)), (mine, other), (spare, near)]
            last += [(other, at(x, o, 1 - x, z ^ 1))]
            for side in range(2):
                inside += [(at(x, side, core, z), at(x, side, 1 - core, z)) for core in range(2)]
            for pairs in (across, direct, relay):
                pairs += [(near, spare), (spare, near)]
        relay += [(at(1, o, 1, z), at(1, o, 1, z - 2)), (at(1, o, 0, z), at(0, o, 0, z))]
        relay += [(at(0, o, 0, z), at(0, o, 1, z)), (at(0, o, 1, z), at(1, o, 0, z))]
    return first, across, far, direct, middle, relay, last, inside


def routed(
    outside,
    inside_head,
    inside_tail,
    inside_pair,
    seq_head,
    seq_tail,
    pair_mask,
    split_weight,
    pair_weight,
    span_blocks,
    partition,
):
    size = outside.shape[1]
    cells = pair_mask.shape[0]
    row_count = lax.axis_size("row")
    first, across, far, direct, middle, relay, last, inside = routes(lax.axis_size("col"))
    code = pltpu.VMEM((size, size), jnp.bfloat16)
    full = pltpu.VMEM((size, size), jnp.float32)
    output = pltpu.HBM((size, size), jnp.float32)

    def send(x, pairs):
        x = lax.ppermute(x, ("row", "col"), pairs)
        return pltpu.with_memory_space_constraint(x, pltpu.VMEM)

    def call(kernel, specs, shape, scratch=()):
        outs = tuple(VMEM for _ in shape) if isinstance(shape, tuple) else VMEM
        return pl.pallas_call(
            kernel,
            in_specs=specs,
            out_specs=outs,
            out_shape=shape,
            scratch_shapes=scratch,
            compiler_params=PARAMS,
        )

    half = pltpu.VMEM((size // 2, size), jnp.bfloat16)
    held, right, top, rest = call(
        right_kernel,
        [HBM] * 2,
        (code, code, half, half),
        [code, pltpu.SemaphoreType.DMA((2,))],
    )(
        pltpu.with_memory_space_constraint(outside, pltpu.HBM),
        pltpu.with_memory_space_constraint(inside_tail, pltpu.HBM),
    )
    q1 = send(right, first)
    qx = send(rest, across)
    qh = send(right, far)
    qa = send(top, direct)
    left, left_code = call(
        functools.partial(left_kernel, row_count), [VMEM] * 2 + [ANY], (full, code)
    )(inside_head, held, right)
    i0 = send(left_code, inside)
    left, moved = call(chip_kernel, [VMEM] * 2, (full, code))(left, i0)
    q4 = send(moved, middle)
    q3 = send(qx, relay)
    pair = call(add_kernel, [VMEM] * 2, code)(right, q1)
    q2 = send(pair, last)
    factor = call(
        factor_kernel,
        [SMEM] + [VMEM] * 3 + [ANY] * 3,
        full,
        [pltpu.SMEM((1,), jnp.int32), pltpu.SMEM((1,), jnp.float32), pltpu.SemaphoreType.DMA((2,))],
    )(pair_weight, seq_head, seq_tail, inside_pair, span_blocks, partition, pair)
    partial, scale = call(
        functools.partial(partial_kernel, row_count),
        [SMEM] * 2 + [VMEM] * 7,
        (full, pltpu.VMEM((cells, size), jnp.float32)),
    )(
        pair_mask,
        split_weight,
        seq_head,
        seq_tail,
        left,
        q4,
        qh,
        qx,
        qa,
    )
    return pl.pallas_call(
        last_kernel,
        in_specs=[VMEM] * 5,
        out_specs=(HBM, HBM),
        out_shape=(output, output),
        scratch_shapes=[full, full, pltpu.SemaphoreType.DMA((2, cells))],
        compiler_params=PARAMS,
    )(scale, partial, factor, q3, q2)


def passed_along(x, axis, by):
    length = lax.axis_size(axis)
    return lax.ppermute(x, axis, [(i, (i + by) % length) for i in range(length)])


def finish(
    right_sum,
    left_sum,
    head_codes,
    tail_codes,
    mask_rows,
    pair_rows,
    split_weight,
    pair_weight,
    span_blocks,
    partition,
    owner_factor,
):
    cycles, tile_size = head_codes.shape
    repeat = tile_size // mask_rows.shape[1]
    allowed = jnp.repeat(
        jnp.repeat(mask_rows.astype(jnp.float32), repeat, axis=0), repeat, axis=1
    ).reshape(cycles, tile_size, tile_size)
    letters = jnp.arange(4, dtype=jnp.int32)
    head_hot = (head_codes[:, :, None] == letters[None, None, :]).astype(jnp.float32)
    tail_hot = (tail_codes[:, :, None] == letters[None, None, :]).astype(jnp.float32)
    head_weight = jnp.einsum("mak,k->ma", head_hot, split_weight, precision=precise)
    tail_weight = jnp.einsum("mak,k->ma", tail_hot, split_weight, precision=precise)
    outside_diag = (
        owner_factor
        * allowed
        * (right_sum * tail_weight[:, None, :] + head_weight[:, :, None] * left_sum)
        / tile_size
    )
    pair_table = jnp.einsum("mak,kl,mbl->mab", head_hot, pair_weight, tail_hot, precision=precise)
    positions = jnp.arange(tile_size, dtype=jnp.float32)
    span_nt = (
        tile_size * span_blocks[0].astype(jnp.float32) + positions[None, :] - positions[:, None]
    )
    penalty = jnp.sqrt(64.0 * tile_size / span_nt)
    pair_prob = (
        pair_rows.reshape(cycles, tile_size, tile_size)
        * outside_diag
        * pair_table
        * penalty[None, :, :]
        / partition[0]
    )
    return (
        outside_diag.reshape(cycles * tile_size, tile_size),
        pair_prob.reshape(cycles * tile_size, tile_size),
    )


def as_tiles(array):
    return array.reshape(-1, array.shape[1], array.shape[1])


def move_later(stack):
    return jnp.concatenate([jnp.zeros_like(stack), stack[:-1]], axis=0)


def general(
    outside,
    inside_head,
    inside_tail,
    inside_pair,
    seq_head,
    seq_tail,
    pair_mask,
    split_weight,
    pair_weight,
    span_blocks,
    partition,
):
    row_count = lax.axis_size("row")
    row_id = lax.axis_index("row")
    col_id = lax.axis_index("col")
    out_tiles = as_tiles(outside)
    right_part = jnp.einsum(
        "mac,mbc->mab", out_tiles, as_tiles(inside_tail), preferred_element_type=jnp.float32
    )
    window = passed_along(right_part, "col", -1)
    for level in range(row_count.bit_length() - 1):
        window = window + passed_along(window, "col", -(1 << level))
    reach = (col_id - row_id) % row_count
    reach = jnp.where(reach == 0, row_count, reach)
    left_part = jnp.einsum(
        "mca,mcb->mab", as_tiles(inside_head), out_tiles, preferred_element_type=jnp.float32
    )
    left_part = jnp.where(col_id < reach, move_later(left_part), left_part)
    left_sum = lax.psum(left_part, "row")
    owner_factor = (row_id == col_id % row_count).astype(jnp.float32)
    return finish(
        window,
        left_sum,
        seq_head,
        seq_tail,
        pair_mask,
        inside_pair,
        split_weight,
        pair_weight,
        span_blocks,
        partition,
        owner_factor,
    )


def per_device(use_routes, outside, *rest):
    return (routed if use_routes else general)(outside, *rest)


def solution(mesh):
    placed = (
        P("row", "col"),
        P("row", "col"),
        P("row", "col"),
        P(None, "col"),
        P(None, "col"),
        P(None, "col"),
        P(None, "col"),
        P(),
        P(),
        P(),
        P(),
    )

    def step(outside, *rest):
        rows, cols = mesh.shape["row"], mesh.shape["col"]
        one_tile = outside.shape[0] // rows == outside.shape[1] // cols
        use_routes = one_tile and rows == 4 and cols % 4 == 0
        body = jax.shard_map(
            lambda *args: per_device(use_routes, *args),
            mesh=mesh,
            in_specs=placed,
            out_specs=(P("row", "col"), P("row", "col")),
            check_vma=False,
        )
        return body(outside, *rest)

    return step
```

```python
import functools

import jax
import jax.numpy as jnp
from jax import lax
from jax.experimental import pallas as pl
from jax.experimental.pallas import tpu as pltpu
from jax.sharding import PartitionSpec as P


precise = lax.Precision.HIGHEST
VMEM = pl.BlockSpec(memory_space=pltpu.VMEM)
SMEM = pl.BlockSpec(memory_space=pltpu.SMEM)
ANY = pl.BlockSpec(memory_space=pl.ANY)
HBM = pl.BlockSpec(memory_space=pltpu.HBM)
CHUNKS = 4
PARAMS = pltpu.CompilerParams(vmem_limit_bytes=16 << 20)


SPLIT = 0.25
GAIN = 2.0**6.2


def encode(x):
    high = x >= SPLIT
    y = x * jnp.where(high, 4.0 / GAIN, 4.0 * GAIN)
    y2 = y * y
    y5 = y2 * y2 * y
    y10 = y5 * y5
    y20 = y10 * y10
    return jnp.where(high, y20, -y20).astype(jnp.bfloat16)


def decode(code):
    y = code.astype(jnp.float32)
    root = jnp.exp2(jnp.log2(jnp.abs(y)) * 0.05)
    return root * jnp.where(y > 0.0, 0.25 * GAIN, 0.25 / GAIN)


def place():
    return lax.axis_index("row"), lax.axis_index("col")


def pick(codes, value, count):
    out = jnp.full(codes.shape, value(0))
    for k in range(1, count):
        out = jnp.where(codes == k, value(k), out)
    return out


def right_kernel(out_hbm, tail_hbm, out_ref, code_ref, top_ref, rest_ref, tail_ref, sems):
    tail = pltpu.make_async_copy(tail_hbm, tail_ref, sems.at[0])
    out = pltpu.make_async_copy(out_hbm, out_ref, sems.at[1])
    tail.start()
    out.start()
    tail.wait()
    out.wait()
    term = lax.dot_general(
        out_ref[...], tail_ref[...], (((1,), (1,)), ((), ())), preferred_element_type=jnp.float32
    )
    code_ref[...] = encode(term * (1.0 / term.shape[0]))
    half = rest_ref.shape[0]
    top_ref[...] = code_ref[pl.ds(0, half), :]
    rest_ref[...] = code_ref[pl.ds(half, half), :]


def left_kernel(rows, head_ref, out_ref, after_ref, left_ref, code_ref):
    term = lax.dot_general(
        head_ref[...], out_ref[...], (((0,), (0,)), ((), ())), preferred_element_type=jnp.float32
    )
    row_id, col_id = place()
    reach = lax.rem(col_id - row_id + 2 * rows, rows)
    reach = jnp.where(reach == 0, rows, reach)
    term = jnp.where(col_id >= reach, term * (1.0 / term.shape[0]), 0.0)
    left_ref[...] = term
    code_ref[...] = encode(term)


def chip_kernel(left_ref, other_ref, left_out_ref, code_ref):
    total = left_ref[...] + decode(other_ref[...])
    left_out_ref[...] = total
    code_ref[...] = encode(total)


def add_kernel(a_ref, b_ref, code_ref):
    code_ref[...] = encode(decode(a_ref[...]) + decode(b_ref[...]))


def masked_row(mask_ref, row, size):
    count = mask_ref.shape[1]
    place = lax.broadcasted_iota(jnp.int32, (1, size), 1) // (size // count)
    return pick(place, lambda k: mask_ref[row, k], count).astype(jnp.float32)


def column(row):
    return jnp.broadcast_to(row, (8, row.shape[1])).T[:, :1]


def factor_kernel(
    weight_ref,
    head_ref,
    tail_ref,
    pair_ref,
    span_hbm,
    partition_hbm,
    after_ref,
    factor_ref,
    span_ref,
    partition_ref,
    sems,
):
    scalars = [
        pltpu.make_async_copy(span_hbm, span_ref, sems.at[0]),
        pltpu.make_async_copy(partition_hbm, partition_ref, sems.at[1]),
    ]
    for copy in scalars:
        copy.start()
    for copy in scalars:
        copy.wait()
    size = pair_ref.shape[0]
    kinds = weight_ref.shape[0]
    step = size // CHUNKS
    tail = tail_ref[...]
    head = column(head_ref[...].astype(jnp.float32)).astype(jnp.int32)
    table = [pick(tail, lambda k, j=j: weight_ref[j, k], kinds) for j in range(kinds)]
    reach = span_ref[0].astype(jnp.float32) * size
    for cell in range(CHUNKS):
        rows = pl.ds(cell * step, step)
        part = slice(cell * step, (cell + 1) * step)
        pairs = jnp.broadcast_to(table[0], (step, size))
        for j in range(1, kinds):
            pairs = jnp.where(head[part] == j, table[j], pairs)
        a = lax.broadcasted_iota(jnp.int32, (step, size), 0) + cell * step
        b = lax.broadcasted_iota(jnp.int32, (step, size), 1)
        span = reach + (b - a).astype(jnp.float32)
        penalty = jnp.sqrt(64.0 * size / span)
        factor_ref[rows, :] = pair_ref[rows, :] * pairs * penalty / partition_ref[0]


def partial_kernel(
    rows_count,
    mask_ref,
    split_ref,
    head_ref,
    tail_ref,
    left_ref,
    middle_ref,
    far_ref,
    across_ref,
    direct_ref,
    partial_ref,
    scale_ref,
):
    size = left_ref.shape[0]
    cells = mask_ref.shape[0]
    step = size // cells
    kinds = split_ref.shape[0]
    row_id, col_id = place()
    is_owner = row_id == lax.rem(col_id, rows_count)
    head = column(head_ref[...].astype(jnp.float32)).astype(jnp.int32)
    tail_weight = pick(tail_ref[...], lambda k: split_ref[k], kinds)
    head_weight = pick(head, lambda k: split_ref[k], kinds)
    for cell in range(cells):
        rows = pl.ds(cell * step, step)
        part = slice(cell * step, (cell + 1) * step)
        if 2 * cell < cells:
            code = direct_ref[rows, :].astype(jnp.float32)
        else:
            code = across_ref[pl.ds((cell - cells // 2) * step, step), :].astype(jnp.float32)
            code = jnp.where(lax.rem(col_id, 2) == 0, code, 0.0)
        allowed = jnp.where(is_owner, masked_row(mask_ref, cell, size), 0.0)
        right = (decode(far_ref[rows, :]) + decode(code)) * tail_weight
        left = (left_ref[rows, :] + decode(middle_ref[rows, :])) * head_weight[part]
        partial_ref[rows, :] = allowed * (right + left)
        scale_ref[pl.ds(cell, 1), :] = allowed * tail_weight


def last_kernel(
    scale_ref,
    partial_ref,
    factor_ref,
    relay_ref,
    last_ref,
    outside_hbm,
    prob_hbm,
    outside_ref,
    prob_ref,
    sems,
):
    _, col_id = place()
    cells = scale_ref.shape[0]
    step = outside_ref.shape[0] // cells
    copies = []
    for cell in range(cells):
        rows = pl.ds(cell * step, step)
        right = decode(last_ref[rows, :])
        if 2 * cell >= cells:
            code = relay_ref[pl.ds((cell - cells // 2) * step, step), :].astype(jnp.float32)
            right += decode(jnp.where(lax.rem(col_id, 2) == 1, code, 0.0))
        total = partial_ref[rows, :] + scale_ref[pl.ds(cell, 1), :] * right
        outside_ref[rows, :] = total
        copies.append(
            pltpu.make_async_copy(
                outside_ref.at[rows, :], outside_hbm.at[rows, :], sems.at[0, cell]
            )
        )
        copies[-1].start()
        prob_ref[rows, :] = total * factor_ref[rows, :]
        copies.append(
            pltpu.make_async_copy(prob_ref.at[rows, :], prob_hbm.at[rows, :], sems.at[1, cell])
        )
        copies[-1].start()
    for copy in copies:
        copy.wait()


def routes(col_count):
    depth = col_count // 2

    def at(x, y, core, z):
        return (2 * y + core) * col_count + 2 * (z % depth) + x

    first, across, far, direct, middle, relay, last, inside = [[] for _ in range(8)]
    for z in range(depth):
        o = z % 2
        n = 1 - o
        for x in range(2):
            mine, other = at(x, o, x, z), at(x, o, 1 - x, z)
            near, spare = at(x, n, x, z), at(x, n, 1 - x, z)
            first += [(mine, other), (other, mine)]
            first += [(spare, at(1 - x, n, 1 - x, z)), (near, spare)]
            across += [(other, at(1 - x, o, 1 - x, z)), (mine, other)]
            far += [(mine, at(x, o, x, z - 2)), (other, spare), (spare, near), (near, other)]
            direct += [(other, at(1 - x, o, 1 - x, z + 2 * x - 2)), (mine, other)]
            middle += [(near, mine), (mine, other), (other, spare), (spare, near)]
            last += [(near, at(x, n, x, z - 1)), (mine, other), (spare, near)]
            last += [(other, at(x, o, 1 - x, z ^ 1))]
            for side in range(2):
                inside += [(at(x, side, core, z), at(x, side, 1 - core, z)) for core in range(2)]
            for pairs in (across, direct, relay):
                pairs += [(near, spare), (spare, near)]
        relay += [(at(1, o, 1, z), at(1, o, 1, z - 2)), (at(1, o, 0, z), at(0, o, 0, z))]
        relay += [(at(0, o, 0, z), at(0, o, 1, z)), (at(0, o, 1, z), at(1, o, 0, z))]
    return first, across, far, direct, middle, relay, last, inside


def routed(
    outside,
    inside_head,
    inside_tail,
    inside_pair,
    seq_head,
    seq_tail,
    pair_mask,
    split_weight,
    pair_weight,
    span_blocks,
    partition,
):
    size = outside.shape[1]
    cells = pair_mask.shape[0]
    row_count = lax.axis_size("row")
    first, across, far, direct, middle, relay, last, inside = routes(lax.axis_size("col"))
    code = pltpu.VMEM((size, size), jnp.bfloat16)
    full = pltpu.VMEM((size, size), jnp.float32)
    output = pltpu.HBM((size, size), jnp.float32)

    def send(x, pairs):
        x = lax.ppermute(x, ("row", "col"), pairs)
        return pltpu.with_memory_space_constraint(x, pltpu.VMEM)

    def call(kernel, specs, shape, scratch=()):
        outs = tuple(VMEM for _ in shape) if isinstance(shape, tuple) else VMEM
        return pl.pallas_call(
            kernel,
            in_specs=specs,
            out_specs=outs,
            out_shape=shape,
            scratch_shapes=scratch,
            compiler_params=PARAMS,
        )

    half = pltpu.VMEM((size // 2, size), jnp.bfloat16)
    held, right, top, rest = call(
        right_kernel,
        [HBM] * 2,
        (code, code, half, half),
        [code, pltpu.SemaphoreType.DMA((2,))],
    )(
        pltpu.with_memory_space_constraint(outside, pltpu.HBM),
        pltpu.with_memory_space_constraint(inside_tail, pltpu.HBM),
    )
    q1 = send(right, first)
    qx = send(rest, across)
    qh = send(right, far)
    qa = send(top, direct)
    left, left_code = call(
        functools.partial(left_kernel, row_count), [VMEM] * 2 + [ANY], (full, code)
    )(inside_head, held, right)
    i0 = send(left_code, inside)
    left, moved = call(chip_kernel, [VMEM] * 2, (full, code))(left, i0)
    q4 = send(moved, middle)
    q3 = send(qx, relay)
    pair = call(add_kernel, [VMEM] * 2, code)(right, q1)
    q2 = send(pair, last)
    factor = call(
        factor_kernel,
        [SMEM] + [VMEM] * 3 + [ANY] * 3,
        full,
        [pltpu.SMEM((1,), jnp.int32), pltpu.SMEM((1,), jnp.float32), pltpu.SemaphoreType.DMA((2,))],
    )(pair_weight, seq_head, seq_tail, inside_pair, span_blocks, partition, pair)
    partial, scale = call(
        functools.partial(partial_kernel, row_count),
        [SMEM] * 2 + [VMEM] * 7,
        (full, pltpu.VMEM((cells, size), jnp.float32)),
    )(
        pair_mask,
        split_weight,
        seq_head,
        seq_tail,
        left,
        q4,
        qh,
        qx,
        qa,
    )
    return pl.pallas_call(
        last_kernel,
        in_specs=[VMEM] * 5,
        out_specs=(HBM, HBM),
        out_shape=(output, output),
        scratch_shapes=[full, full, pltpu.SemaphoreType.DMA((2, cells))],
        compiler_params=PARAMS,
    )(scale, partial, factor, q3, q2)


def passed_along(x, axis, by):
    length = lax.axis_size(axis)
    return lax.ppermute(x, axis, [(i, (i + by) % length) for i in range(length)])


def finish(
    right_sum,
    left_sum,
    head_codes,
    tail_codes,
    mask_rows,
    pair_rows,
    split_weight,
    pair_weight,
    span_blocks,
    partition,
    owner_factor,
):
    cycles, tile_size = head_codes.shape
    repeat = tile_size // mask_rows.shape[1]
    allowed = jnp.repeat(
        jnp.repeat(mask_rows.astype(jnp.float32), repeat, axis=0), repeat, axis=1
    ).reshape(cycles, tile_size, tile_size)
    letters = jnp.arange(4, dtype=jnp.int32)
    head_hot = (head_codes[:, :, None] == letters[None, None, :]).astype(jnp.float32)
    tail_hot = (tail_codes[:, :, None] == letters[None, None, :]).astype(jnp.float32)
    head_weight = jnp.einsum("mak,k->ma", head_hot, split_weight, precision=precise)
    tail_weight = jnp.einsum("mak,k->ma", tail_hot, split_weight, precision=precise)
    outside_diag = (
        owner_factor
        * allowed
        * (right_sum * tail_weight[:, None, :] + head_weight[:, :, None] * left_sum)
        / tile_size
    )
    pair_table = jnp.einsum("mak,kl,mbl->mab", head_hot, pair_weight, tail_hot, precision=precise)
    positions = jnp.arange(tile_size, dtype=jnp.float32)
    span_nt = (
        tile_size * span_blocks[0].astype(jnp.float32) + positions[None, :] - positions[:, None]
    )
    penalty = jnp.sqrt(64.0 * tile_size / span_nt)
    pair_prob = (
        pair_rows.reshape(cycles, tile_size, tile_size)
        * outside_diag
        * pair_table
        * penalty[None, :, :]
        / partition[0]
    )
    return (
        outside_diag.reshape(cycles * tile_size, tile_size),
        pair_prob.reshape(cycles * tile_size, tile_size),
    )


def as_tiles(array):
    return array.reshape(-1, array.shape[1], array.shape[1])


def move_later(stack):
    return jnp.concatenate([jnp.zeros_like(stack), stack[:-1]], axis=0)


def general(
    outside,
    inside_head,
    inside_tail,
    inside_pair,
    seq_head,
    seq_tail,
    pair_mask,
    split_weight,
    pair_weight,
    span_blocks,
    partition,
):
    row_count = lax.axis_size("row")
    row_id = lax.axis_index("row")
    col_id = lax.axis_index("col")
    out_tiles = as_tiles(outside)
    right_part = jnp.einsum(
        "mac,mbc->mab", out_tiles, as_tiles(inside_tail), preferred_element_type=jnp.float32
    )
    window = passed_along(right_part, "col", -1)
    for level in range(row_count.bit_length() - 1):
        window = window + passed_along(window, "col", -(1 << level))
    reach = (col_id - row_id) % row_count
    reach = jnp.where(reach == 0, row_count, reach)
    left_part = jnp.einsum(
        "mca,mcb->mab", as_tiles(inside_head), out_tiles, preferred_element_type=jnp.float32
    )
    left_part = jnp.where(col_id < reach, move_later(left_part), left_part)
    left_sum = lax.psum(left_part, "row")
    owner_factor = (row_id == col_id % row_count).astype(jnp.float32)
    return finish(
        window,
        left_sum,
        seq_head,
        seq_tail,
        pair_mask,
        inside_pair,
        split_weight,
        pair_weight,
        span_blocks,
        partition,
        owner_factor,
    )


def per_device(use_routes, outside, *rest):
    return (routed if use_routes else general)(outside, *rest)


def solution(mesh):
    placed = (
        P("row", "col"),
        P("row", "col"),
        P("row", "col"),
        P(None, "col"),
        P(None, "col"),
        P(None, "col"),
        P(None, "col"),
        P(),
        P(),
        P(),
        P(),
    )

    def step(outside, *rest):
        rows, cols = mesh.shape["row"], mesh.shape["col"]
        one_tile = outside.shape[0] // rows == outside.shape[1] // cols
        use_routes = one_tile and rows == 4 and cols % 4 == 0
        body = jax.shard_map(
            lambda *args: per_device(use_routes, *args),
            mesh=mesh,
            in_specs=placed,
            out_specs=(P("row", "col"), P("row", "col")),
            check_vma=False,
        )
        return body(outside, *rest)

    return step
```

```python
import functools

import jax
import jax.numpy as jnp
from jax import lax
from jax.experimental import pallas as pl
from jax.experimental.pallas import tpu as pltpu
from jax.sharding import PartitionSpec as P


precise = lax.Precision.HIGHEST
VMEM = pl.BlockSpec(memory_space=pltpu.VMEM)
SMEM = pl.BlockSpec(memory_space=pltpu.SMEM)
ANY = pl.BlockSpec(memory_space=pl.ANY)
HBM = pl.BlockSpec(memory_space=pltpu.HBM)
CHUNKS = 4
PARAMS = pltpu.CompilerParams(vmem_limit_bytes=16 << 20)


SPLIT = 0.25
GAIN = 2.0**5.9


def encode(x, scale=1.0):
    y = x * jnp.where(x >= SPLIT / scale, scale * 4.0 / GAIN, scale * -4.0 * GAIN)
    y2 = y * y
    y5 = y2 * y2 * y
    y10 = y5 * y5
    return (y10 * y10 * y).astype(jnp.bfloat16)


def decode(code):
    y = code.astype(jnp.float32)
    root = jnp.exp2(jnp.log2(jnp.abs(y)) * (1.0 / 21.0))
    return root * jnp.where(y > 0.0, 0.25 * GAIN, 0.25 / GAIN)


def place():
    return lax.axis_index("row"), lax.axis_index("col")


def pick(codes, value, count):
    out = jnp.full(codes.shape, value(0))
    for k in range(1, count):
        out = jnp.where(codes == k, value(k), out)
    return out


def right_kernel(out_hbm, tail_hbm, out_ref, code_ref, top_ref, rest_ref, tail_ref, sems):
    tail = pltpu.make_async_copy(tail_hbm, tail_ref, sems.at[0])
    out = pltpu.make_async_copy(out_hbm, out_ref, sems.at[1])
    tail.start()
    out.start()
    tail.wait()
    out.wait()
    term = lax.dot_general(
        out_ref[...], tail_ref[...], (((1,), (1,)), ((), ())), preferred_element_type=jnp.float32
    )
    half = top_ref.shape[0]
    for part, part_ref in ((pl.ds(0, half), top_ref), (pl.ds(half, half), rest_ref)):
        code = encode(term[part.start : part.start + half], 1.0 / term.shape[0])
        code_ref[part, :] = code
        part_ref[...] = code


def left_kernel(rows, head_ref, out_ref, after_ref, left_ref, code_ref):
    term = lax.dot_general(
        head_ref[...], out_ref[...], (((0,), (0,)), ((), ())), preferred_element_type=jnp.float32
    )
    row_id, col_id = place()
    reach = lax.rem(col_id - row_id + 2 * rows, rows)
    reach = jnp.where(reach == 0, rows, reach)
    term = jnp.where(col_id >= reach, term * (1.0 / term.shape[0]), 0.0)
    left_ref[...] = term
    code_ref[...] = encode(term)


def chip_kernel(left_ref, other_ref, left_out_ref, code_ref):
    total = left_ref[...] + decode(other_ref[...])
    left_out_ref[...] = total
    code_ref[...] = encode(total)


def add_kernel(a_ref, b_ref, code_ref):
    code_ref[...] = encode(decode(a_ref[...]) + decode(b_ref[...]))


def masked_row(mask_ref, row, size):
    count = mask_ref.shape[1]
    place = lax.broadcasted_iota(jnp.int32, (1, size), 1) // (size // count)
    return pick(place, lambda k: mask_ref[row, k], count).astype(jnp.float32)


def column(row):
    return jnp.broadcast_to(row, (8, row.shape[1])).T[:, :1]


def factor_kernel(
    weight_ref,
    head_ref,
    tail_ref,
    pair_ref,
    span_hbm,
    partition_hbm,
    after_ref,
    factor_ref,
    span_ref,
    partition_ref,
    sems,
):
    scalars = [
        pltpu.make_async_copy(span_hbm, span_ref, sems.at[0]),
        pltpu.make_async_copy(partition_hbm, partition_ref, sems.at[1]),
    ]
    for copy in scalars:
        copy.start()
    for copy in scalars:
        copy.wait()
    size = pair_ref.shape[0]
    kinds = weight_ref.shape[0]
    step = size // CHUNKS
    tail = tail_ref[...]
    head = column(head_ref[...].astype(jnp.float32)).astype(jnp.int32)
    table = [pick(tail, lambda k, j=j: weight_ref[j, k], kinds) for j in range(kinds)]
    reach = span_ref[0].astype(jnp.float32) * size
    for cell in range(CHUNKS):
        rows = pl.ds(cell * step, step)
        part = slice(cell * step, (cell + 1) * step)
        pairs = jnp.broadcast_to(table[0], (step, size))
        for j in range(1, kinds):
            pairs = jnp.where(head[part] == j, table[j], pairs)
        a = lax.broadcasted_iota(jnp.int32, (step, size), 0) + cell * step
        b = lax.broadcasted_iota(jnp.int32, (step, size), 1)
        span = reach + (b - a).astype(jnp.float32)
        penalty = jnp.sqrt(64.0 * size / span)
        factor_ref[rows, :] = pair_ref[rows, :] * pairs * penalty / partition_ref[0]


def partial_kernel(
    rows_count,
    mask_ref,
    split_ref,
    head_ref,
    tail_ref,
    left_ref,
    middle_ref,
    far_ref,
    across_ref,
    direct_ref,
    partial_ref,
    scale_ref,
):
    size = left_ref.shape[0]
    cells = mask_ref.shape[0]
    step = size // cells
    kinds = split_ref.shape[0]
    row_id, col_id = place()
    is_owner = row_id == lax.rem(col_id, rows_count)
    head = column(head_ref[...].astype(jnp.float32)).astype(jnp.int32)
    tail_weight = pick(tail_ref[...], lambda k: split_ref[k], kinds)
    head_weight = pick(head, lambda k: split_ref[k], kinds)
    for cell in range(cells):
        rows = pl.ds(cell * step, step)
        part = slice(cell * step, (cell + 1) * step)
        if 2 * cell < cells:
            code = direct_ref[rows, :].astype(jnp.float32)
        else:
            code = across_ref[pl.ds((cell - cells // 2) * step, step), :].astype(jnp.float32)
            code = jnp.where(lax.rem(col_id, 2) == 0, code, 0.0)
        allowed = jnp.where(is_owner, masked_row(mask_ref, cell, size), 0.0)
        right = (decode(far_ref[rows, :]) + decode(code)) * tail_weight
        left = (left_ref[rows, :] + decode(middle_ref[rows, :])) * head_weight[part]
        partial_ref[rows, :] = allowed * (right + left)
        scale_ref[pl.ds(cell, 1), :] = allowed * tail_weight


def last_kernel(
    scale_ref,
    partial_ref,
    factor_ref,
    relay_ref,
    last_ref,
    outside_hbm,
    prob_hbm,
    outside_ref,
    prob_ref,
    sems,
):
    _, col_id = place()
    cells = scale_ref.shape[0]
    step = outside_ref.shape[0] // cells
    copies = []
    for cell in range(cells):
        rows = pl.ds(cell * step, step)
        right = decode(last_ref[rows, :])
        if 2 * cell >= cells:
            code = relay_ref[pl.ds((cell - cells // 2) * step, step), :].astype(jnp.float32)
            right += decode(jnp.where(lax.rem(col_id, 2) == 1, code, 0.0))
        total = partial_ref[rows, :] + scale_ref[pl.ds(cell, 1), :] * right
        outside_ref[rows, :] = total
        copies.append(
            pltpu.make_async_copy(
                outside_ref.at[rows, :], outside_hbm.at[rows, :], sems.at[0, cell]
            )
        )
        copies[-1].start()
        prob_ref[rows, :] = total * factor_ref[rows, :]
        copies.append(
            pltpu.make_async_copy(prob_ref.at[rows, :], prob_hbm.at[rows, :], sems.at[1, cell])
        )
        copies[-1].start()
    for copy in copies:
        copy.wait()


def routes(col_count):
    depth = col_count // 2

    def at(x, y, core, z):
        return (2 * y + core) * col_count + 2 * (z % depth) + x

    first, across, far, direct, middle, relay, last, inside = [[] for _ in range(8)]
    for z in range(depth):
        o = z % 2
        n = 1 - o
        for x in range(2):
            mine, other = at(x, o, x, z), at(x, o, 1 - x, z)
            near, spare = at(x, n, x, z), at(x, n, 1 - x, z)
            first += [(mine, other), (other, mine)]
            first += [(spare, at(1 - x, n, 1 - x, z)), (near, spare)]
            across += [(other, at(1 - x, o, 1 - x, z)), (mine, other)]
            far += [(mine, at(x, o, x, z - 2)), (other, spare), (spare, near), (near, other)]
            direct += [(other, at(1 - x, o, 1 - x, z + 2 * x - 2)), (mine, other)]
            middle += [(near, mine), (mine, other), (other, spare), (spare, near)]
            last += [(near, at(x, n, x, z - 1)), (mine, other), (spare, near)]
            last += [(other, at(x, o, 1 - x, z ^ 1))]
            for side in range(2):
                inside += [(at(x, side, core, z), at(x, side, 1 - core, z)) for core in range(2)]
            for pairs in (across, direct, relay):
                pairs += [(near, spare), (spare, near)]
        relay += [(at(1, o, 1, z), at(1, o, 1, z - 2)), (at(1, o, 0, z), at(0, o, 0, z))]
        relay += [(at(0, o, 0, z), at(0, o, 1, z)), (at(0, o, 1, z), at(1, o, 0, z))]
    return first, across, far, direct, middle, relay, last, inside


def routed(
    outside,
    inside_head,
    inside_tail,
    inside_pair,
    seq_head,
    seq_tail,
    pair_mask,
    split_weight,
    pair_weight,
    span_blocks,
    partition,
):
    size = outside.shape[1]
    cells = pair_mask.shape[0]
    row_count = lax.axis_size("row")
    first, across, far, direct, middle, relay, last, inside = routes(lax.axis_size("col"))
    code = pltpu.VMEM((size, size), jnp.bfloat16)
    full = pltpu.VMEM((size, size), jnp.float32)
    output = pltpu.HBM((size, size), jnp.float32)

    def send(x, pairs):
        x = lax.ppermute(x, ("row", "col"), pairs)
        return pltpu.with_memory_space_constraint(x, pltpu.VMEM)

    def call(kernel, specs, shape, scratch=()):
        outs = tuple(VMEM for _ in shape) if isinstance(shape, tuple) else VMEM
        return pl.pallas_call(
            kernel,
            in_specs=specs,
            out_specs=outs,
            out_shape=shape,
            scratch_shapes=scratch,
            compiler_params=PARAMS,
        )

    half = pltpu.VMEM((size // 2, size), jnp.bfloat16)
    held, right, top, rest = call(
        right_kernel,
        [HBM] * 2,
        (code, code, half, half),
        [code, pltpu.SemaphoreType.DMA((2,))],
    )(
        pltpu.with_memory_space_constraint(outside, pltpu.HBM),
        pltpu.with_memory_space_constraint(inside_tail, pltpu.HBM),
    )
    q1 = send(right, first)
    qx = send(rest, across)
    qh = send(right, far)
    qa = send(top, direct)
    left, left_code = call(
        functools.partial(left_kernel, row_count), [VMEM] * 2 + [ANY], (full, code)
    )(inside_head, held, right)
    i0 = send(left_code, inside)
    left, moved = call(chip_kernel, [VMEM] * 2, (full, code))(left, i0)
    q4 = send(moved, middle)
    q3 = send(qx, relay)
    pair = call(add_kernel, [VMEM] * 2, code)(right, q1)
    q2 = send(pair, last)
    factor = call(
        factor_kernel,
        [SMEM] + [VMEM] * 3 + [ANY] * 3,
        full,
        [pltpu.SMEM((1,), jnp.int32), pltpu.SMEM((1,), jnp.float32), pltpu.SemaphoreType.DMA((2,))],
    )(pair_weight, seq_head, seq_tail, inside_pair, span_blocks, partition, pair)
    partial, scale = call(
        functools.partial(partial_kernel, row_count),
        [SMEM] * 2 + [VMEM] * 7,
        (full, pltpu.VMEM((cells, size), jnp.float32)),
    )(
        pair_mask,
        split_weight,
        seq_head,
        seq_tail,
        left,
        q4,
        qh,
        qx,
        qa,
    )
    return pl.pallas_call(
        last_kernel,
        in_specs=[VMEM] * 5,
        out_specs=(HBM, HBM),
        out_shape=(output, output),
        scratch_shapes=[full, full, pltpu.SemaphoreType.DMA((2, cells))],
        compiler_params=PARAMS,
    )(scale, partial, factor, q3, q2)


def passed_along(x, axis, by):
    length = lax.axis_size(axis)
    return lax.ppermute(x, axis, [(i, (i + by) % length) for i in range(length)])


def finish(
    right_sum,
    left_sum,
    head_codes,
    tail_codes,
    mask_rows,
    pair_rows,
    split_weight,
    pair_weight,
    span_blocks,
    partition,
    owner_factor,
):
    cycles, tile_size = head_codes.shape
    repeat = tile_size // mask_rows.shape[1]
    allowed = jnp.repeat(
        jnp.repeat(mask_rows.astype(jnp.float32), repeat, axis=0), repeat, axis=1
    ).reshape(cycles, tile_size, tile_size)
    letters = jnp.arange(4, dtype=jnp.int32)
    head_hot = (head_codes[:, :, None] == letters[None, None, :]).astype(jnp.float32)
    tail_hot = (tail_codes[:, :, None] == letters[None, None, :]).astype(jnp.float32)
    head_weight = jnp.einsum("mak,k->ma", head_hot, split_weight, precision=precise)
    tail_weight = jnp.einsum("mak,k->ma", tail_hot, split_weight, precision=precise)
    outside_diag = (
        owner_factor
        * allowed
        * (right_sum * tail_weight[:, None, :] + head_weight[:, :, None] * left_sum)
        / tile_size
    )
    pair_table = jnp.einsum("mak,kl,mbl->mab", head_hot, pair_weight, tail_hot, precision=precise)
    positions = jnp.arange(tile_size, dtype=jnp.float32)
    span_nt = (
        tile_size * span_blocks[0].astype(jnp.float32) + positions[None, :] - positions[:, None]
    )
    penalty = jnp.sqrt(64.0 * tile_size / span_nt)
    pair_prob = (
        pair_rows.reshape(cycles, tile_size, tile_size)
        * outside_diag
        * pair_table
        * penalty[None, :, :]
        / partition[0]
    )
    return (
        outside_diag.reshape(cycles * tile_size, tile_size),
        pair_prob.reshape(cycles * tile_size, tile_size),
    )


def as_tiles(array):
    return array.reshape(-1, array.shape[1], array.shape[1])


def move_later(stack):
    return jnp.concatenate([jnp.zeros_like(stack), stack[:-1]], axis=0)


def general(
    outside,
    inside_head,
    inside_tail,
    inside_pair,
    seq_head,
    seq_tail,
    pair_mask,
    split_weight,
    pair_weight,
    span_blocks,
    partition,
):
    row_count = lax.axis_size("row")
    row_id = lax.axis_index("row")
    col_id = lax.axis_index("col")
    out_tiles = as_tiles(outside)
    right_part = jnp.einsum(
        "mac,mbc->mab", out_tiles, as_tiles(inside_tail), preferred_element_type=jnp.float32
    )
    window = passed_along(right_part, "col", -1)
    for level in range(row_count.bit_length() - 1):
        window = window + passed_along(window, "col", -(1 << level))
    reach = (col_id - row_id) % row_count
    reach = jnp.where(reach == 0, row_count, reach)
    left_part = jnp.einsum(
        "mca,mcb->mab", as_tiles(inside_head), out_tiles, preferred_element_type=jnp.float32
    )
    left_part = jnp.where(col_id < reach, move_later(left_part), left_part)
    left_sum = lax.psum(left_part, "row")
    owner_factor = (row_id == col_id % row_count).astype(jnp.float32)
    return finish(
        window,
        left_sum,
        seq_head,
        seq_tail,
        pair_mask,
        inside_pair,
        split_weight,
        pair_weight,
        span_blocks,
        partition,
        owner_factor,
    )


def per_device(use_routes, outside, *rest):
    return (routed if use_routes else general)(outside, *rest)


def solution(mesh):
    placed = (
        P("row", "col"),
        P("row", "col"),
        P("row", "col"),
        P(None, "col"),
        P(None, "col"),
        P(None, "col"),
        P(None, "col"),
        P(),
        P(),
        P(),
        P(),
    )

    def step(outside, *rest):
        rows, cols = mesh.shape["row"], mesh.shape["col"]
        one_tile = outside.shape[0] // rows == outside.shape[1] // cols
        use_routes = one_tile and rows == 4 and cols % 4 == 0
        body = jax.shard_map(
            lambda *args: per_device(use_routes, *args),
            mesh=mesh,
            in_specs=placed,
            out_specs=(P("row", "col"), P("row", "col")),
            check_vma=False,
        )
        return body(outside, *rest)

    return step
```

```python
import functools

import jax
import jax.numpy as jnp
from jax import lax
from jax.experimental import pallas as pl
from jax.experimental.pallas import tpu as pltpu
from jax.sharding import PartitionSpec as P


precise = lax.Precision.HIGHEST
VMEM = pl.BlockSpec(memory_space=pltpu.VMEM)
SMEM = pl.BlockSpec(memory_space=pltpu.SMEM)
ANY = pl.BlockSpec(memory_space=pl.ANY)
HBM = pl.BlockSpec(memory_space=pltpu.HBM)
CHUNKS = 4
PARAMS = pltpu.CompilerParams(vmem_limit_bytes=16 << 20)


SPLIT = 0.25
GAIN = 2.0**5.9


def encode(x, scale=1.0):
    y = x * jnp.where(x >= SPLIT / scale, scale * 4.0 / GAIN, scale * -4.0 * GAIN)
    y2 = y * y
    y5 = y2 * y2 * y
    y10 = y5 * y5
    return (y10 * y10 * y).astype(jnp.bfloat16)


def decode(code):
    y = code.astype(jnp.float32)
    root = jnp.exp2(jnp.log2(jnp.abs(y)) * (1.0 / 21.0))
    return root * jnp.where(y > 0.0, 0.25 * GAIN, 0.25 / GAIN)


def place():
    return lax.axis_index("row"), lax.axis_index("col")


def pick(codes, value, count):
    out = jnp.full(codes.shape, value(0))
    for k in range(1, count):
        out = jnp.where(codes == k, value(k), out)
    return out


def right_kernel(out_hbm, tail_hbm, out_ref, code_ref, top_ref, rest_ref, tail_ref, sems):
    tail = pltpu.make_async_copy(tail_hbm, tail_ref, sems.at[0])
    out = pltpu.make_async_copy(out_hbm, out_ref, sems.at[1])
    tail.start()
    out.start()
    tail.wait()
    out.wait()
    term = lax.dot_general(
        out_ref[...], tail_ref[...], (((1,), (1,)), ((), ())), preferred_element_type=jnp.float32
    )
    half = top_ref.shape[0]
    for part, part_ref in ((pl.ds(0, half), top_ref), (pl.ds(half, half), rest_ref)):
        code = encode(term[part.start : part.start + half], 1.0 / term.shape[0])
        code_ref[part, :] = code
        part_ref[...] = code


def left_kernel(rows, head_ref, out_ref, after_ref, left_ref, code_ref):
    term = lax.dot_general(
        head_ref[...], out_ref[...], (((0,), (0,)), ((), ())), preferred_element_type=jnp.float32
    )
    row_id, col_id = place()
    reach = lax.rem(col_id - row_id + 2 * rows, rows)
    reach = jnp.where(reach == 0, rows, reach)
    term = jnp.where(col_id >= reach, term * (1.0 / term.shape[0]), 0.0)
    left_ref[...] = term
    code_ref[...] = encode(term)


def chip_kernel(left_ref, other_ref, left_out_ref, code_ref):
    total = left_ref[...] + decode(other_ref[...])
    left_out_ref[...] = total
    code_ref[...] = encode(total)


def own_kernel(code_ref, after_ref, value_ref):
    value_ref[...] = decode(code_ref[...])


def add_kernel(own_ref, code_ref, sum_ref):
    sum_ref[...] = encode(own_ref[...] + decode(code_ref[...]))


def masked_row(mask_ref, row, size):
    count = mask_ref.shape[1]
    place = lax.broadcasted_iota(jnp.int32, (1, size), 1) // (size // count)
    return pick(place, lambda k: mask_ref[row, k], count).astype(jnp.float32)


def column(row):
    return jnp.broadcast_to(row, (8, row.shape[1])).T[:, :1]


def factor_kernel(
    weight_ref,
    head_ref,
    tail_ref,
    pair_ref,
    span_hbm,
    partition_hbm,
    after_ref,
    factor_ref,
    span_ref,
    partition_ref,
    sems,
):
    scalars = [
        pltpu.make_async_copy(span_hbm, span_ref, sems.at[0]),
        pltpu.make_async_copy(partition_hbm, partition_ref, sems.at[1]),
    ]
    for copy in scalars:
        copy.start()
    for copy in scalars:
        copy.wait()
    size = pair_ref.shape[0]
    kinds = weight_ref.shape[0]
    step = size // CHUNKS
    tail = tail_ref[...]
    head = column(head_ref[...].astype(jnp.float32)).astype(jnp.int32)
    table = [pick(tail, lambda k, j=j: weight_ref[j, k], kinds) for j in range(kinds)]
    reach = span_ref[0].astype(jnp.float32) * size
    for cell in range(CHUNKS):
        rows = pl.ds(cell * step, step)
        part = slice(cell * step, (cell + 1) * step)
        pairs = jnp.broadcast_to(table[0], (step, size))
        for j in range(1, kinds):
            pairs = jnp.where(head[part] == j, table[j], pairs)
        a = lax.broadcasted_iota(jnp.int32, (step, size), 0) + cell * step
        b = lax.broadcasted_iota(jnp.int32, (step, size), 1)
        span = reach + (b - a).astype(jnp.float32)
        penalty = jnp.sqrt(64.0 * size / span)
        factor_ref[rows, :] = pair_ref[rows, :] * pairs * penalty / partition_ref[0]


def partial_kernel(
    rows_count,
    mask_ref,
    split_ref,
    head_ref,
    tail_ref,
    left_ref,
    middle_ref,
    far_ref,
    across_ref,
    direct_ref,
    partial_ref,
    scale_ref,
):
    size = left_ref.shape[0]
    cells = mask_ref.shape[0]
    step = size // cells
    kinds = split_ref.shape[0]
    row_id, col_id = place()
    is_owner = row_id == lax.rem(col_id, rows_count)
    head = column(head_ref[...].astype(jnp.float32)).astype(jnp.int32)
    tail_weight = pick(tail_ref[...], lambda k: split_ref[k], kinds)
    head_weight = pick(head, lambda k: split_ref[k], kinds)
    for cell in range(cells):
        rows = pl.ds(cell * step, step)
        part = slice(cell * step, (cell + 1) * step)
        if 2 * cell < cells:
            code = direct_ref[rows, :].astype(jnp.float32)
        else:
            code = across_ref[pl.ds((cell - cells // 2) * step, step), :].astype(jnp.float32)
            code = jnp.where(lax.rem(col_id, 2) == 0, code, 0.0)
        allowed = jnp.where(is_owner, masked_row(mask_ref, cell, size), 0.0)
        right = (decode(far_ref[rows, :]) + decode(code)) * tail_weight
        left = (left_ref[rows, :] + decode(middle_ref[rows, :])) * head_weight[part]
        partial_ref[rows, :] = allowed * (right + left)
        scale_ref[pl.ds(cell, 1), :] = allowed * tail_weight


def last_kernel(
    scale_ref,
    partial_ref,
    factor_ref,
    relay_ref,
    last_ref,
    outside_hbm,
    prob_hbm,
    outside_ref,
    prob_ref,
    sems,
):
    _, col_id = place()
    cells = scale_ref.shape[0]
    step = outside_ref.shape[0] // cells
    copies = []
    for cell in range(cells):
        rows = pl.ds(cell * step, step)
        right = decode(last_ref[rows, :])
        if 2 * cell >= cells:
            code = relay_ref[pl.ds((cell - cells // 2) * step, step), :].astype(jnp.float32)
            right += decode(jnp.where(lax.rem(col_id, 2) == 1, code, 0.0))
        total = partial_ref[rows, :] + scale_ref[pl.ds(cell, 1), :] * right
        outside_ref[rows, :] = total
        copies.append(
            pltpu.make_async_copy(
                outside_ref.at[rows, :], outside_hbm.at[rows, :], sems.at[0, cell]
            )
        )
        copies[-1].start()
        prob_ref[rows, :] = total * factor_ref[rows, :]
        copies.append(
            pltpu.make_async_copy(prob_ref.at[rows, :], prob_hbm.at[rows, :], sems.at[1, cell])
        )
        copies[-1].start()
    for copy in copies:
        copy.wait()


def routes(col_count):
    depth = col_count // 2

    def at(x, y, core, z):
        return (2 * y + core) * col_count + 2 * (z % depth) + x

    first, across, far, direct, middle, relay, last, inside = [[] for _ in range(8)]
    for z in range(depth):
        o = z % 2
        n = 1 - o
        for x in range(2):
            mine, other = at(x, o, x, z), at(x, o, 1 - x, z)
            near, spare = at(x, n, x, z), at(x, n, 1 - x, z)
            first += [(mine, other), (other, mine)]
            first += [(spare, at(1 - x, n, 1 - x, z)), (near, spare)]
            across += [(other, at(1 - x, o, 1 - x, z)), (mine, other)]
            far += [(mine, at(x, o, x, z - 2)), (other, spare), (spare, near), (near, other)]
            direct += [(other, at(1 - x, o, 1 - x, z + 2 * x - 2)), (mine, other)]
            middle += [(near, mine), (mine, other), (other, spare), (spare, near)]
            last += [(near, at(x, n, x, z - 1)), (mine, other), (spare, near)]
            last += [(other, at(x, o, 1 - x, z ^ 1))]
            for side in range(2):
                inside += [(at(x, side, core, z), at(x, side, 1 - core, z)) for core in range(2)]
            for pairs in (across, direct, relay):
                pairs += [(near, spare), (spare, near)]
        relay += [(at(1, o, 1, z), at(1, o, 1, z - 2)), (at(1, o, 0, z), at(0, o, 0, z))]
        relay += [(at(0, o, 0, z), at(0, o, 1, z)), (at(0, o, 1, z), at(1, o, 0, z))]
    return first, across, far, direct, middle, relay, last, inside


def routed(
    outside,
    inside_head,
    inside_tail,
    inside_pair,
    seq_head,
    seq_tail,
    pair_mask,
    split_weight,
    pair_weight,
    span_blocks,
    partition,
):
    size = outside.shape[1]
    cells = pair_mask.shape[0]
    row_count = lax.axis_size("row")
    first, across, far, direct, middle, relay, last, inside = routes(lax.axis_size("col"))
    code = pltpu.VMEM((size, size), jnp.bfloat16)
    full = pltpu.VMEM((size, size), jnp.float32)
    output = pltpu.HBM((size, size), jnp.float32)

    def send(x, pairs):
        x = lax.ppermute(x, ("row", "col"), pairs)
        return pltpu.with_memory_space_constraint(x, pltpu.VMEM)

    def call(kernel, specs, shape, scratch=()):
        outs = tuple(VMEM for _ in shape) if isinstance(shape, tuple) else VMEM
        return pl.pallas_call(
            kernel,
            in_specs=specs,
            out_specs=outs,
            out_shape=shape,
            scratch_shapes=scratch,
            compiler_params=PARAMS,
        )

    half = pltpu.VMEM((size // 2, size), jnp.bfloat16)
    held, right, top, rest = call(
        right_kernel,
        [HBM] * 2,
        (code, code, half, half),
        [code, pltpu.SemaphoreType.DMA((2,))],
    )(
        pltpu.with_memory_space_constraint(outside, pltpu.HBM),
        pltpu.with_memory_space_constraint(inside_tail, pltpu.HBM),
    )
    q1 = send(right, first)
    qx = send(rest, across)
    qh = send(right, far)
    qa = send(top, direct)
    left, left_code = call(
        functools.partial(left_kernel, row_count), [VMEM] * 2 + [ANY], (full, code)
    )(inside_head, held, right)
    i0 = send(left_code, inside)
    left, moved = call(chip_kernel, [VMEM] * 2, (full, code))(left, i0)
    q4 = send(moved, middle)
    q3 = send(qx, relay)
    own = call(own_kernel, [VMEM, ANY], full)(right, moved)
    pair = call(add_kernel, [VMEM] * 2, code)(own, q1)
    q2 = send(pair, last)
    factor = call(
        factor_kernel,
        [SMEM] + [VMEM] * 3 + [ANY] * 3,
        full,
        [pltpu.SMEM((1,), jnp.int32), pltpu.SMEM((1,), jnp.float32), pltpu.SemaphoreType.DMA((2,))],
    )(pair_weight, seq_head, seq_tail, inside_pair, span_blocks, partition, pair)
    partial, scale = call(
        functools.partial(partial_kernel, row_count),
        [SMEM] * 2 + [VMEM] * 7,
        (full, pltpu.VMEM((cells, size), jnp.float32)),
    )(
        pair_mask,
        split_weight,
        seq_head,
        seq_tail,
        left,
        q4,
        qh,
        qx,
        qa,
    )
    return pl.pallas_call(
        last_kernel,
        in_specs=[VMEM] * 5,
        out_specs=(HBM, HBM),
        out_shape=(output, output),
        scratch_shapes=[full, full, pltpu.SemaphoreType.DMA((2, cells))],
        compiler_params=PARAMS,
    )(scale, partial, factor, q3, q2)


def passed_along(x, axis, by):
    length = lax.axis_size(axis)
    return lax.ppermute(x, axis, [(i, (i + by) % length) for i in range(length)])


def finish(
    right_sum,
    left_sum,
    head_codes,
    tail_codes,
    mask_rows,
    pair_rows,
    split_weight,
    pair_weight,
    span_blocks,
    partition,
    owner_factor,
):
    cycles, tile_size = head_codes.shape
    repeat = tile_size // mask_rows.shape[1]
    allowed = jnp.repeat(
        jnp.repeat(mask_rows.astype(jnp.float32), repeat, axis=0), repeat, axis=1
    ).reshape(cycles, tile_size, tile_size)
    letters = jnp.arange(4, dtype=jnp.int32)
    head_hot = (head_codes[:, :, None] == letters[None, None, :]).astype(jnp.float32)
    tail_hot = (tail_codes[:, :, None] == letters[None, None, :]).astype(jnp.float32)
    head_weight = jnp.einsum("mak,k->ma", head_hot, split_weight, precision=precise)
    tail_weight = jnp.einsum("mak,k->ma", tail_hot, split_weight, precision=precise)
    outside_diag = (
        owner_factor
        * allowed
        * (right_sum * tail_weight[:, None, :] + head_weight[:, :, None] * left_sum)
        / tile_size
    )
    pair_table = jnp.einsum("mak,kl,mbl->mab", head_hot, pair_weight, tail_hot, precision=precise)
    positions = jnp.arange(tile_size, dtype=jnp.float32)
    span_nt = (
        tile_size * span_blocks[0].astype(jnp.float32) + positions[None, :] - positions[:, None]
    )
    penalty = jnp.sqrt(64.0 * tile_size / span_nt)
    pair_prob = (
        pair_rows.reshape(cycles, tile_size, tile_size)
        * outside_diag
        * pair_table
        * penalty[None, :, :]
        / partition[0]
    )
    return (
        outside_diag.reshape(cycles * tile_size, tile_size),
        pair_prob.reshape(cycles * tile_size, tile_size),
    )


def as_tiles(array):
    return array.reshape(-1, array.shape[1], array.shape[1])


def move_later(stack):
    return jnp.concatenate([jnp.zeros_like(stack), stack[:-1]], axis=0)


def general(
    outside,
    inside_head,
    inside_tail,
    inside_pair,
    seq_head,
    seq_tail,
    pair_mask,
    split_weight,
    pair_weight,
    span_blocks,
    partition,
):
    row_count = lax.axis_size("row")
    row_id = lax.axis_index("row")
    col_id = lax.axis_index("col")
    out_tiles = as_tiles(outside)
    right_part = jnp.einsum(
        "mac,mbc->mab", out_tiles, as_tiles(inside_tail), preferred_element_type=jnp.float32
    )
    window = passed_along(right_part, "col", -1)
    for level in range(row_count.bit_length() - 1):
        window = window + passed_along(window, "col", -(1 << level))
    reach = (col_id - row_id) % row_count
    reach = jnp.where(reach == 0, row_count, reach)
    left_part = jnp.einsum(
        "mca,mcb->mab", as_tiles(inside_head), out_tiles, preferred_element_type=jnp.float32
    )
    left_part = jnp.where(col_id < reach, move_later(left_part), left_part)
    left_sum = lax.psum(left_part, "row")
    owner_factor = (row_id == col_id % row_count).astype(jnp.float32)
    return finish(
        window,
        left_sum,
        seq_head,
        seq_tail,
        pair_mask,
        inside_pair,
        split_weight,
        pair_weight,
        span_blocks,
        partition,
        owner_factor,
    )


def per_device(use_routes, outside, *rest):
    return (routed if use_routes else general)(outside, *rest)


def solution(mesh):
    placed = (
        P("row", "col"),
        P("row", "col"),
        P("row", "col"),
        P(None, "col"),
        P(None, "col"),
        P(None, "col"),
        P(None, "col"),
        P(),
        P(),
        P(),
        P(),
    )

    def step(outside, *rest):
        rows, cols = mesh.shape["row"], mesh.shape["col"]
        one_tile = outside.shape[0] // rows == outside.shape[1] // cols
        use_routes = one_tile and rows == 4 and cols % 4 == 0
        body = jax.shard_map(
            lambda *args: per_device(use_routes, *args),
            mesh=mesh,
            in_specs=placed,
            out_specs=(P("row", "col"), P("row", "col")),
            check_vma=False,
        )
        return body(outside, *rest)

    return step
```

```python
import functools

import jax
import jax.numpy as jnp
from jax import lax
from jax.experimental import pallas as pl
from jax.experimental.pallas import tpu as pltpu
from jax.sharding import PartitionSpec as P


precise = lax.Precision.HIGHEST
VMEM = pl.BlockSpec(memory_space=pltpu.VMEM)
SMEM = pl.BlockSpec(memory_space=pltpu.SMEM)
ANY = pl.BlockSpec(memory_space=pl.ANY)
HBM = pl.BlockSpec(memory_space=pltpu.HBM)
CHUNKS = 4
PARAMS = pltpu.CompilerParams(vmem_limit_bytes=16 << 20)


SPLIT = 0.25
GAIN = 2.0**5.9


def encode(x, scale=1.0):
    y = x * jnp.where(x >= SPLIT / scale, scale * 4.0 / GAIN, scale * -4.0 * GAIN)
    y2 = y * y
    y5 = y2 * y2 * y
    y10 = y5 * y5
    return (y10 * y10 * y).astype(jnp.bfloat16)


def decode(code):
    y = code.astype(jnp.float32)
    root = jnp.exp2(jnp.log2(jnp.abs(y)) * (1.0 / 21.0))
    return root * jnp.where(y > 0.0, 0.25 * GAIN, 0.25 / GAIN)


def place():
    return lax.axis_index("row"), lax.axis_index("col")


def pick(codes, value, count):
    out = jnp.full(codes.shape, value(0))
    for k in range(1, count):
        out = jnp.where(codes == k, value(k), out)
    return out


def right_kernel(out_hbm, tail_hbm, out_ref, code_ref, top_ref, rest_ref, tail_ref, sems):
    tail = pltpu.make_async_copy(tail_hbm, tail_ref, sems.at[0])
    out = pltpu.make_async_copy(out_hbm, out_ref, sems.at[1])
    tail.start()
    out.start()
    tail.wait()
    out.wait()
    term = lax.dot_general(
        out_ref[...], tail_ref[...], (((1,), (1,)), ((), ())), preferred_element_type=jnp.float32
    )
    half = top_ref.shape[0]
    for part, part_ref in ((pl.ds(0, half), top_ref), (pl.ds(half, half), rest_ref)):
        code = encode(term[part.start : part.start + half], 1.0 / term.shape[0])
        code_ref[part, :] = code
        part_ref[...] = code


def left_kernel(rows, head_ref, out_ref, after_ref, left_ref, code_ref):
    term = lax.dot_general(
        head_ref[...], out_ref[...], (((0,), (0,)), ((), ())), preferred_element_type=jnp.float32
    )
    row_id, col_id = place()
    reach = lax.rem(col_id - row_id + 2 * rows, rows)
    reach = jnp.where(reach == 0, rows, reach)
    term = jnp.where(col_id >= reach, term * (1.0 / term.shape[0]), 0.0)
    left_ref[...] = term
    code_ref[...] = encode(term)


def chip_kernel(left_ref, other_ref, left_out_ref, code_ref):
    total = left_ref[...] + decode(other_ref[...])
    left_out_ref[...] = total
    code_ref[...] = encode(total)


def own_kernel(code_ref, after_ref, value_ref):
    value_ref[...] = decode(code_ref[...])


def add_kernel(own_ref, code_ref, sum_ref):
    sum_ref[...] = encode(own_ref[...] + decode(code_ref[...]))


def masked_row(mask_ref, row, size):
    count = mask_ref.shape[1]
    place = lax.broadcasted_iota(jnp.int32, (1, size), 1) // (size // count)
    return pick(place, lambda k: mask_ref[row, k], count).astype(jnp.float32)


def column(row):
    return jnp.broadcast_to(row, (8, row.shape[1])).T[:, :1]


def factor_kernel(
    weight_ref,
    head_ref,
    tail_ref,
    pair_ref,
    span_hbm,
    partition_hbm,
    after_ref,
    factor_ref,
    span_ref,
    partition_ref,
    sems,
):
    scalars = [
        pltpu.make_async_copy(span_hbm, span_ref, sems.at[0]),
        pltpu.make_async_copy(partition_hbm, partition_ref, sems.at[1]),
    ]
    for copy in scalars:
        copy.start()
    for copy in scalars:
        copy.wait()
    size = pair_ref.shape[0]
    kinds = weight_ref.shape[0]
    step = size // CHUNKS
    tail = tail_ref[...]
    head = column(head_ref[...].astype(jnp.float32)).astype(jnp.int32)
    table = [pick(tail, lambda k, j=j: weight_ref[j, k], kinds) for j in range(kinds)]
    reach = span_ref[0].astype(jnp.float32) * size
    for cell in range(CHUNKS):
        rows = pl.ds(cell * step, step)
        part = slice(cell * step, (cell + 1) * step)
        pairs = jnp.broadcast_to(table[0], (step, size))
        for j in range(1, kinds):
            pairs = jnp.where(head[part] == j, table[j], pairs)
        a = lax.broadcasted_iota(jnp.int32, (step, size), 0) + cell * step
        b = lax.broadcasted_iota(jnp.int32, (step, size), 1)
        span = reach + (b - a).astype(jnp.float32)
        penalty = jnp.sqrt(64.0 * size / span)
        factor_ref[rows, :] = pair_ref[rows, :] * pairs * penalty / partition_ref[0]


def partial_kernel(
    rows_count,
    mask_ref,
    split_ref,
    head_ref,
    tail_ref,
    left_ref,
    middle_ref,
    far_ref,
    across_ref,
    direct_ref,
    partial_ref,
    scale_ref,
):
    size = left_ref.shape[0]
    cells = mask_ref.shape[0]
    step = size // cells
    kinds = split_ref.shape[0]
    row_id, col_id = place()
    is_owner = row_id == lax.rem(col_id, rows_count)
    head = column(head_ref[...].astype(jnp.float32)).astype(jnp.int32)
    tail_weight = pick(tail_ref[...], lambda k: split_ref[k], kinds)
    head_weight = pick(head, lambda k: split_ref[k], kinds)
    for cell in range(cells):
        rows = pl.ds(cell * step, step)
        part = slice(cell * step, (cell + 1) * step)
        if 2 * cell < cells:
            code = direct_ref[rows, :].astype(jnp.float32)
        else:
            code = across_ref[pl.ds((cell - cells // 2) * step, step), :].astype(jnp.float32)
            code = jnp.where(lax.rem(col_id, 2) == 0, code, 0.0)
        allowed = jnp.where(is_owner, masked_row(mask_ref, cell, size), 0.0)
        right = (decode(far_ref[rows, :]) + decode(code)) * tail_weight
        left = (left_ref[rows, :] + decode(middle_ref[rows, :])) * head_weight[part]
        partial_ref[rows, :] = allowed * (right + left)
        scale_ref[pl.ds(cell, 1), :] = allowed * tail_weight


def last_kernel(
    scale_ref,
    partial_ref,
    factor_ref,
    relay_ref,
    last_ref,
    outside_hbm,
    prob_hbm,
    outside_ref,
    prob_ref,
    sems,
):
    _, col_id = place()
    cells = scale_ref.shape[0]
    step = outside_ref.shape[0] // cells
    copies = []
    groups = [(0, step // 2), (step // 2, step - step // 2)]
    groups += [(cell * step, step) for cell in range(1, cells)]
    for group, (begin, count) in enumerate(groups):
        cell = begin // step
        rows = pl.ds(begin, count)
        right = decode(last_ref[rows, :])
        if 2 * cell >= cells:
            code = relay_ref[pl.ds(begin - cells // 2 * step, count), :].astype(jnp.float32)
            right += decode(jnp.where(lax.rem(col_id, 2) == 1, code, 0.0))
        total = partial_ref[rows, :] + scale_ref[pl.ds(cell, 1), :] * right
        outside_ref[rows, :] = total
        copies.append(
            pltpu.make_async_copy(
                outside_ref.at[rows, :], outside_hbm.at[rows, :], sems.at[0, group]
            )
        )
        copies[-1].start()
        prob_ref[rows, :] = total * factor_ref[rows, :]
        copies.append(
            pltpu.make_async_copy(prob_ref.at[rows, :], prob_hbm.at[rows, :], sems.at[1, group])
        )
        copies[-1].start()
    for copy in copies:
        copy.wait()


def routes(col_count):
    depth = col_count // 2

    def at(x, y, core, z):
        return (2 * y + core) * col_count + 2 * (z % depth) + x

    first, across, far, direct, middle, relay, last, inside = [[] for _ in range(8)]
    for z in range(depth):
        o = z % 2
        n = 1 - o
        for x in range(2):
            mine, other = at(x, o, x, z), at(x, o, 1 - x, z)
            near, spare = at(x, n, x, z), at(x, n, 1 - x, z)
            first += [(mine, other), (other, mine)]
            first += [(spare, at(1 - x, n, 1 - x, z)), (near, spare)]
            across += [(other, at(1 - x, o, 1 - x, z)), (mine, other)]
            far += [(mine, at(x, o, x, z - 2)), (other, spare), (spare, near), (near, other)]
            direct += [(other, at(1 - x, o, 1 - x, z + 2 * x - 2)), (mine, other)]
            middle += [(near, mine), (mine, other), (other, spare), (spare, near)]
            last += [(near, at(x, n, x, z - 1)), (mine, other), (spare, near)]
            last += [(other, at(x, o, 1 - x, z ^ 1))]
            for side in range(2):
                inside += [(at(x, side, core, z), at(x, side, 1 - core, z)) for core in range(2)]
            for pairs in (across, direct, relay):
                pairs += [(near, spare), (spare, near)]
        relay += [(at(1, o, 1, z), at(1, o, 1, z - 2)), (at(1, o, 0, z), at(0, o, 0, z))]
        relay += [(at(0, o, 0, z), at(0, o, 1, z)), (at(0, o, 1, z), at(1, o, 0, z))]
    return first, across, far, direct, middle, relay, last, inside


def routed(
    outside,
    inside_head,
    inside_tail,
    inside_pair,
    seq_head,
    seq_tail,
    pair_mask,
    split_weight,
    pair_weight,
    span_blocks,
    partition,
):
    size = outside.shape[1]
    cells = pair_mask.shape[0]
    row_count = lax.axis_size("row")
    first, across, far, direct, middle, relay, last, inside = routes(lax.axis_size("col"))
    code = pltpu.VMEM((size, size), jnp.bfloat16)
    full = pltpu.VMEM((size, size), jnp.float32)
    output = pltpu.HBM((size, size), jnp.float32)

    def send(x, pairs):
        x = lax.ppermute(x, ("row", "col"), pairs)
        return pltpu.with_memory_space_constraint(x, pltpu.VMEM)

    def call(kernel, specs, shape, scratch=()):
        outs = tuple(VMEM for _ in shape) if isinstance(shape, tuple) else VMEM
        return pl.pallas_call(
            kernel,
            in_specs=specs,
            out_specs=outs,
            out_shape=shape,
            scratch_shapes=scratch,
            compiler_params=PARAMS,
        )

    half = pltpu.VMEM((size // 2, size), jnp.bfloat16)
    held, right, top, rest = call(
        right_kernel,
        [HBM] * 2,
        (code, code, half, half),
        [code, pltpu.SemaphoreType.DMA((2,))],
    )(
        pltpu.with_memory_space_constraint(outside, pltpu.HBM),
        pltpu.with_memory_space_constraint(inside_tail, pltpu.HBM),
    )
    q1 = send(right, first)
    qx = send(rest, across)
    qh = send(right, far)
    qa = send(top, direct)
    left, left_code = call(
        functools.partial(left_kernel, row_count), [VMEM] * 2 + [ANY], (full, code)
    )(inside_head, held, right)
    i0 = send(left_code, inside)
    left, moved = call(chip_kernel, [VMEM] * 2, (full, code))(left, i0)
    q4 = send(moved, middle)
    q3 = send(qx, relay)
    own = call(own_kernel, [VMEM, ANY], full)(right, moved)
    pair = call(add_kernel, [VMEM] * 2, code)(own, q1)
    q2 = send(pair, last)
    factor = call(
        factor_kernel,
        [SMEM] + [VMEM] * 3 + [ANY] * 3,
        full,
        [pltpu.SMEM((1,), jnp.int32), pltpu.SMEM((1,), jnp.float32), pltpu.SemaphoreType.DMA((2,))],
    )(pair_weight, seq_head, seq_tail, inside_pair, span_blocks, partition, pair)
    partial, scale = call(
        functools.partial(partial_kernel, row_count),
        [SMEM] * 2 + [VMEM] * 7,
        (full, pltpu.VMEM((cells, size), jnp.float32)),
    )(
        pair_mask,
        split_weight,
        seq_head,
        seq_tail,
        left,
        q4,
        qh,
        qx,
        qa,
    )
    return pl.pallas_call(
        last_kernel,
        in_specs=[VMEM] * 5,
        out_specs=(HBM, HBM),
        out_shape=(output, output),
        scratch_shapes=[full, full, pltpu.SemaphoreType.DMA((2, cells + 1))],
        compiler_params=PARAMS,
    )(scale, partial, factor, q3, q2)


def passed_along(x, axis, by):
    length = lax.axis_size(axis)
    return lax.ppermute(x, axis, [(i, (i + by) % length) for i in range(length)])


def finish(
    right_sum,
    left_sum,
    head_codes,
    tail_codes,
    mask_rows,
    pair_rows,
    split_weight,
    pair_weight,
    span_blocks,
    partition,
    owner_factor,
):
    cycles, tile_size = head_codes.shape
    repeat = tile_size // mask_rows.shape[1]
    allowed = jnp.repeat(
        jnp.repeat(mask_rows.astype(jnp.float32), repeat, axis=0), repeat, axis=1
    ).reshape(cycles, tile_size, tile_size)
    letters = jnp.arange(4, dtype=jnp.int32)
    head_hot = (head_codes[:, :, None] == letters[None, None, :]).astype(jnp.float32)
    tail_hot = (tail_codes[:, :, None] == letters[None, None, :]).astype(jnp.float32)
    head_weight = jnp.einsum("mak,k->ma", head_hot, split_weight, precision=precise)
    tail_weight = jnp.einsum("mak,k->ma", tail_hot, split_weight, precision=precise)
    outside_diag = (
        owner_factor
        * allowed
        * (right_sum * tail_weight[:, None, :] + head_weight[:, :, None] * left_sum)
        / tile_size
    )
    pair_table = jnp.einsum("mak,kl,mbl->mab", head_hot, pair_weight, tail_hot, precision=precise)
    positions = jnp.arange(tile_size, dtype=jnp.float32)
    span_nt = (
        tile_size * span_blocks[0].astype(jnp.float32) + positions[None, :] - positions[:, None]
    )
    penalty = jnp.sqrt(64.0 * tile_size / span_nt)
    pair_prob = (
        pair_rows.reshape(cycles, tile_size, tile_size)
        * outside_diag
        * pair_table
        * penalty[None, :, :]
        / partition[0]
    )
    return (
        outside_diag.reshape(cycles * tile_size, tile_size),
        pair_prob.reshape(cycles * tile_size, tile_size),
    )


def as_tiles(array):
    return array.reshape(-1, array.shape[1], array.shape[1])


def move_later(stack):
    return jnp.concatenate([jnp.zeros_like(stack), stack[:-1]], axis=0)


def general(
    outside,
    inside_head,
    inside_tail,
    inside_pair,
    seq_head,
    seq_tail,
    pair_mask,
    split_weight,
    pair_weight,
    span_blocks,
    partition,
):
    row_count = lax.axis_size("row")
    row_id = lax.axis_index("row")
    col_id = lax.axis_index("col")
    out_tiles = as_tiles(outside)
    right_part = jnp.einsum(
        "mac,mbc->mab", out_tiles, as_tiles(inside_tail), preferred_element_type=jnp.float32
    )
    window = passed_along(right_part, "col", -1)
    for level in range(row_count.bit_length() - 1):
        window = window + passed_along(window, "col", -(1 << level))
    reach = (col_id - row_id) % row_count
    reach = jnp.where(reach == 0, row_count, reach)
    left_part = jnp.einsum(
        "mca,mcb->mab", as_tiles(inside_head), out_tiles, preferred_element_type=jnp.float32
    )
    left_part = jnp.where(col_id < reach, move_later(left_part), left_part)
    left_sum = lax.psum(left_part, "row")
    owner_factor = (row_id == col_id % row_count).astype(jnp.float32)
    return finish(
        window,
        left_sum,
        seq_head,
        seq_tail,
        pair_mask,
        inside_pair,
        split_weight,
        pair_weight,
        span_blocks,
        partition,
        owner_factor,
    )


def per_device(use_routes, outside, *rest):
    return (routed if use_routes else general)(outside, *rest)


def solution(mesh):
    placed = (
        P("row", "col"),
        P("row", "col"),
        P("row", "col"),
        P(None, "col"),
        P(None, "col"),
        P(None, "col"),
        P(None, "col"),
        P(),
        P(),
        P(),
        P(),
    )

    def step(outside, *rest):
        rows, cols = mesh.shape["row"], mesh.shape["col"]
        one_tile = outside.shape[0] // rows == outside.shape[1] // cols
        use_routes = one_tile and rows == 4 and cols % 4 == 0
        body = jax.shard_map(
            lambda *args: per_device(use_routes, *args),
            mesh=mesh,
            in_specs=placed,
            out_specs=(P("row", "col"), P("row", "col")),
            check_vma=False,
        )
        return body(outside, *rest)

    return step
```
